128 devices in a mesh: layer: 2 (over core), rows: 64 (over y, x, z).
Axes of the slice: x: 4, y: 4, z: 4, core: 2. Of those that a mesh axis runs over, the one named last changes fastest.
Arguments:
- frames: bfloat16 [3, 4, 128, 64, 128], P(None, None, 'rows'), may hold values from -6 to 6
- hidden_in: bfloat16 [4, 4, 128, 64, 128], P('layer', None, 'rows'), may hold values from -4 to 4
- cell_in: bfloat16 [4, 4, 128, 64, 128], P('layer', None, 'rows'), may hold values from -6 to 6
- memory_in: bfloat16 [4, 128, 64, 128], P(None, 'rows'), may hold values from -6 to 6
- w_x: bfloat16 [4, 576, 448], P('layer'), may hold values from -0.25 to 0.25
- w_h: bfloat16 [4, 576, 256], P('layer'), may hold values from -0.25 to 0.25
- w_m: bfloat16 [4, 576, 192], P('layer'), may hold values from -0.25 to 0.25
- w_o: bfloat16 [4, 1152, 64], P('layer'), may hold values from -0.1875 to 0.1875
- w_last: bfloat16 [4, 128, 64], P('layer'), may hold values from -0.5 to 0.5
Outputs:
- hidden_out: bfloat16 [4, 4, 128, 64, 128], P('layer', None, 'rows')
- cell_out: bfloat16 [4, 4, 128, 64, 128], P('layer', None, 'rows')
- memory_out: bfloat16 [2, 4, 128, 64, 128], P('layer', None, 'rows')
The draws below stay inside these ranges and needn't reach their ends.
All inputs are finite; a program needn't handle non-finite values.
Results may differ from the reference program's by a relative error of at most 0.014.
Values may be sent and summed in bfloat16 or wider, within the bound.
No kernel may reach another device: no remote copies, remote signals or barrier semaphores. Data moves between devices by JAX's collectives and lax.ppermute only.
A program may use at most 64 MiB of HBM per device.

```python
import jax
import jax.numpy as jnp
from jax import lax

CH = 64
GW = 128
SEQS = 4
STEPS = 3
LAYERS = 4
GH = 128


def level_of(rng, shape, cuts, low, top_value):
    def one(position, parts):
        steps = jax.random.uniform(jax.random.fold_in(jax.random.fold_in(rng, 6), position), (parts,), jnp.float32, low / len(cuts), top_value / len(cuts))
        return jnp.repeat(jnp.exp(steps), shape[position] // parts).reshape((-1,) + (1,) * (len(shape) - position - 1))

    factor_of = one(*cuts[0])
    for cut in cuts[1:]:
        factor_of = factor_of * one(*cut)
    return factor_of


def centred(key, extent, spread, reach, cuts=(), kind=jnp.bfloat16):
    result = spread * jax.random.normal(key, extent, jnp.float32)
    if cuts:
        result = result * level_of(key, extent, cuts, -0.22, 0.18)
    return jnp.clip(result, -reach, reach).astype(kind)


def setup_inputs(seed: int = 0) -> dict:
    key_list = jax.random.split(jax.random.key(seed), 10)
    return {
        "frames": centred(key_list[0], (STEPS, SEQS, GH, CH, GW), 1.0, 6.0, ((2, 64),)),
        "hidden_in": centred(key_list[1], (LAYERS, SEQS, GH, CH, GW), 0.7, 4.0, ((0, 2), (2, 64))),
        "cell_in": centred(key_list[2], (LAYERS, SEQS, GH, CH, GW), 1.0, 6.0, ((0, 2), (2, 64))),
        "memory_in": centred(key_list[3], (SEQS, GH, CH, GW), 1.0, 6.0, ((1, 64),)),
        "w_x": centred(key_list[4], (LAYERS, 9 * CH, 7 * CH), (9 * CH) ** -0.5, 0.25, ((0, 2),)),
        "w_h": centred(key_list[5], (LAYERS, 9 * CH, 4 * CH), (9 * CH) ** -0.5, 0.25, ((0, 2),)),
        "w_m": centred(key_list[6], (LAYERS, 9 * CH, 3 * CH), (9 * CH) ** -0.5, 0.25, ((0, 2),)),
        "w_o": centred(key_list[7], (LAYERS, 18 * CH, CH), (18 * CH) ** -0.5, 0.1875, ((0, 2),)),
        "w_last": centred(key_list[8], (LAYERS, 2 * CH, CH), (2 * CH) ** -0.5, 0.5, ((0, 2),)),
    }


def shifted_taps(padded, height):
    pieces = []
    for row_offset in range(3):
        row_band = padded[:, row_offset:row_offset + height]
        zero_column = jnp.zeros_like(row_band[..., :1])
        pieces.append(jnp.concatenate([zero_column, row_band[..., :-1]], axis=-1))
        pieces.append(row_band)
        pieces.append(jnp.concatenate([row_band[..., 1:], zero_column], axis=-1))
    return jnp.concatenate(pieces, axis=2)


def convolve(padded, weight, height):
    taps = shifted_taps(padded, height).astype(jnp.float32)
    return jnp.einsum("ko,brkw->brow", weight.astype(jnp.float32), taps, precision=lax.Precision.HIGHEST)


def gate_math(input_gates, hidden_gates, memory_gates, cell_prev, memory_prev):
    parts_x = jnp.split(input_gates, 7, axis=2)
    parts_h = jnp.split(hidden_gates, 4, axis=2)
    parts_m = jnp.split(memory_gates, 3, axis=2)
    cell_new = (jax.nn.sigmoid(parts_x[1] + parts_h[1] + 1.0) * cell_prev.astype(jnp.float32)
                + jax.nn.sigmoid(parts_x[0] + parts_h[0]) * jnp.tanh(parts_x[2] + parts_h[2])).astype(jnp.bfloat16)
    memory_new = (jax.nn.sigmoid(parts_x[4] + parts_m[1] + 1.0) * memory_prev.astype(jnp.float32)
                  + jax.nn.sigmoid(parts_x[3] + parts_m[0]) * jnp.tanh(parts_x[5] + parts_m[2])).astype(jnp.bfloat16)
    return cell_new, memory_new, parts_x[6] + parts_h[3]


def pad_rows(field):
    return jnp.pad(field, ((0, 0), (1, 1), (0, 0), (0, 0)))


def reference_cell(layer_input, hidden_prev, cell_prev, memory_prev, weight_x, weight_h, weight_m, weight_o, weight_last):
    height = layer_input.shape[1]
    input_gates = convolve(pad_rows(layer_input), weight_x, height)
    hidden_gates = convolve(pad_rows(hidden_prev), weight_h, height)
    memory_gates = convolve(pad_rows(memory_prev), weight_m, height)
    cell_new, memory_new, output_part = gate_math(input_gates, hidden_gates, memory_gates, cell_prev, memory_prev)
    memory_pair = jnp.concatenate([cell_new, memory_new], axis=2)
    output_gate = jax.nn.sigmoid(output_part + convolve(pad_rows(memory_pair), weight_o, height))
    mixed = jnp.einsum("ko,brkw->brow", weight_last.astype(jnp.float32), memory_pair.astype(jnp.float32), precision=lax.Precision.HIGHEST)
    hidden_new = (output_gate * jnp.tanh(mixed)).astype(jnp.bfloat16)
    return hidden_new, cell_new, memory_new


def reference(frames, hidden_in, cell_in, memory_in, w_x, w_h, w_m, w_o, w_last):
    hidden_list = [hidden_in[layer_index] for layer_index in range(LAYERS)]
    cell_list = [cell_in[layer_index] for layer_index in range(LAYERS)]
    memory_now = memory_in
    top_list = []
    for time_index in range(STEPS):
        layer_input = frames[time_index]
        for layer_index in range(LAYERS):
            hidden_new, cell_new, memory_now = reference_cell(
                layer_input, hidden_list[layer_index], cell_list[layer_index], memory_now,
                w_x[layer_index], w_h[layer_index], w_m[layer_index], w_o[layer_index], w_last[layer_index])
            hidden_list[layer_index] = hidden_new
            cell_list[layer_index] = cell_new
            layer_input = hidden_new
            if time_index == STEPS - 1 and layer_index % 2 == 1:
                top_list.append(memory_now)
    return jnp.stack(hidden_list), jnp.stack(cell_list), jnp.stack(top_list)
```

```python
import functools

import jax
import jax.numpy as jnp
from jax import lax
from jax.experimental import pallas as pl
from jax.experimental.pallas import tpu as pltpu
from jax.sharding import PartitionSpec as P

CH = 64
GW = 128
OWN = 4
BF = jnp.bfloat16
F32 = jnp.float32

RUN = {"HT": (0, 4), "M": (4, 4), "HB": (8, 4), "CB": (12, 3), "CT": (15, 1)}
RUN_UNITS = 16
FIRST_A = {"HT": (0, 2), "M": (2, 4), "HB": (6, 4), "CB": (10, 3), "CT": (13, 1), "F0": (14, 4)}
FIRST_B = {"HT": (0, 2), "HB": (2, 4), "CB": (6, 3), "CT": (9, 1), "F1": (10, 4), "F2": (14, 4)}


def sigmoid(v):
    return 0.5 * jnp.tanh(0.5 * v) + 0.5


def taps_of(row):
    lane = lax.broadcasted_iota(jnp.int32, row.shape, 1)
    zero = jnp.zeros_like(row)
    before = jnp.where(lane == 0, zero, pltpu.roll(row, 1, 1))
    after = jnp.where(lane == GW - 1, zero, pltpu.roll(row, GW - 1, 1))
    return jnp.concatenate([before, row, after], axis=0)


def phase_kernel(plan, last, *refs):
    names = plan["names"]
    n_in = len(names)
    ref = dict(zip(names, refs[:n_in]))
    rest = list(refs[n_in:])
    state_out = rest.pop(0)
    if not last:
        near_out = rest.pop(0)
        far_out = rest.pop(0)
    tx, th, tm, tx2, th2, tm2, yb, ob = rest
    core = ref["sc"][0]
    top = ref["sc"][1]
    first_core = core == 0

    def valid(row):
        g = top + row
        return jnp.logical_and(g >= 0, g < 128)

    def keep(row, value):
        return jnp.where(valid(row), value, jnp.zeros_like(value))

    def fetch(field, row):
        own, (near, far, offset, count) = plan["fields"][field]
        if 0 <= row < OWN:
            return ref[own[0]][own[1], row] if own[1] is not None else ref[own[0]][row]
        if row < 0:
            unit = offset + count + row
            value = jnp.where(first_core, ref[far][unit], ref[near][unit])
        else:
            unit = offset + row - OWN
            value = jnp.where(first_core, ref[near][unit], ref[far][unit])
        return keep(row, value)

    def fill(buf, field, reach):
        for i, row in enumerate(range(-reach, OWN + reach)):
            buf[i] = taps_of(fetch(field, row))

    def cell(index, reach, bx, bh, bm, cell_prev, memory_prev, on_cell, on_memory, on_hidden, bm_next):
        w1 = ref["w1"][index]
        w2 = ref["w2"][index]
        wo = ref["wo"][index]
        rows = list(range(-reach, OWN + reach))
        for q in range(0, len(rows), 2):
            cols_1, cols_2 = [], []
            for i in (q, q + 1):
                x_part = [bx[i + a] for a in range(3)]
                cols_1.append(jnp.concatenate(x_part + [bh[i + a] for a in range(3)], axis=0))
                cols_2.append(jnp.concatenate(x_part + [bm[i + a] for a in range(3)], axis=0))
            acc1 = jnp.dot(w1, jnp.concatenate(cols_1, axis=1), preferred_element_type=F32)
            acc2 = jnp.dot(w2, jnp.concatenate(cols_2, axis=1), preferred_element_type=F32)
            c_prev = jnp.concatenate([cell_prev(rows[q]), cell_prev(rows[q + 1])], axis=1).astype(F32)
            m_prev = jnp.concatenate([memory_prev(rows[q]), memory_prev(rows[q + 1])], axis=1).astype(F32)
            c_new = sigmoid(acc1[64:128] + 1.0) * c_prev + sigmoid(acc1[0:64]) * jnp.tanh(acc1[128:192])
            m_new = sigmoid(acc2[64:128] + 1.0) * m_prev + sigmoid(acc2[0:64]) * jnp.tanh(acc2[128:192])
            c_new = c_new.astype(BF)
            m_new = m_new.astype(BF)
            ob[:, q * GW : (q + 2) * GW] = acc1[192:256]
            pair = []
            for j in range(2):
                row = rows[q + j]
                c_row = c_new[:, j * GW : (j + 1) * GW]
                m_row = m_new[:, j * GW : (j + 1) * GW]
                if not 0 <= row < OWN:
                    c_row = keep(row, c_row)
                    m_row = keep(row, m_row)
                on_cell(row, c_row)
                on_memory(row, m_row)
                m_taps = taps_of(m_row)
                if bm_next is not None:
                    bm_next[q + j] = m_taps
                pair.append(jnp.concatenate([taps_of(c_row), m_taps], axis=0))
            yb[:, q * GW : (q + 2) * GW] = jnp.dot(
                wo, jnp.concatenate(pair, axis=1), preferred_element_type=F32
            )
        for q in range(1, len(rows) - 1):
            lanes = slice(q * GW, (q + 1) * GW)
            gate = (
                ob[:, lanes]
                + yb[0:64, (q - 1) * GW : q * GW]
                + yb[64:128, lanes]
                + yb[128:192, (q + 1) * GW : (q + 2) * GW]
            )
            h_new = (sigmoid(gate) * jnp.tanh(yb[192:256, lanes])).astype(BF)
            row = rows[q]
            if not 0 <= row < OWN:
                h_new = keep(row, h_new)
            on_hidden(row, h_new)

    fill(tx, "X", 4)
    fill(th, "HB", 4)
    fill(tm, "M", 4)
    fill(th2, "HT", 2)

    def put(slot):
        def store(row, value):
            if 0 <= row < OWN:
                state_out[slot, row] = value

        return store

    def hidden_first(row, value):
        tx2[row + 2] = taps_of(value)
        if 0 <= row < OWN:
            state_out[0, row] = value

    def nothing(row, value):
        del row, value

    cell(
        0, 3, tx, th, tm,
        lambda row: fetch("CB", row),
        lambda row: fetch("M", row),
        put(2), nothing, hidden_first, tm2,
    )
    tm2_in = tm2.at[1:9]
    cell(
        1, 1, tx2, th2, tm2_in,
        lambda row: fetch("CT", row),
        lambda row: tm2[row + 3, 64:128],
        put(3), put(4), put(1), None,
    )
    if not last:
        for field, slot in (("HT", 1), ("M", 4), ("HB", 0), ("CB", 2), ("CT", 3)):
            offset, count = RUN[field]
            for u in range(count):
                low = state_out[slot, u]
                high = state_out[slot, OWN - count + u]
                near_out[offset + u] = jnp.where(first_core, high, low)
                far_out[offset + u] = jnp.where(first_core, low, high)


def run_phase(operands, plan, last):
    names = list(operands)
    plan = dict(plan, names=names)
    unit = (CH, GW)
    out_shape = [jax.ShapeDtypeStruct((5, OWN) + unit, BF)]
    if not last:
        out_shape += [jax.ShapeDtypeStruct((RUN_UNITS,) + unit, BF)] * 2
    in_specs = [
        pl.BlockSpec(memory_space=pltpu.SMEM if name == "sc" else pltpu.VMEM) for name in names
    ]
    out_specs = [pl.BlockSpec(memory_space=pltpu.VMEM) for _ in out_shape]
    return pl.pallas_call(
        functools.partial(phase_kernel, plan, last),
        out_shape=out_shape,
        in_specs=in_specs,
        out_specs=out_specs,
        scratch_shapes=[
            pltpu.VMEM((12, 3 * CH, GW), BF),
            pltpu.VMEM((12, 3 * CH, GW), BF),
            pltpu.VMEM((12, 3 * CH, GW), BF),
            pltpu.VMEM((8, 3 * CH, GW), BF),
            pltpu.VMEM((8, 3 * CH, GW), BF),
            pltpu.VMEM((10, 3 * CH, GW), BF),
            pltpu.VMEM((4 * CH, 10 * GW), F32),
            pltpu.VMEM((CH, 10 * GW), F32),
        ],
        compiler_params=pltpu.CompilerParams(vmem_limit_bytes=24 << 20),
        name="two_layers_last" if last else "two_layers",
    )(*[operands[name] for name in names])


def prepare_weights(w_x, w_h, w_m, w_o, w_last):
    layers = w_x.shape[0]
    x = jnp.swapaxes(w_x, 1, 2)
    x_c = jnp.concatenate([x[:, 0:192], x[:, 384:448]], axis=1)
    w1 = jnp.concatenate([x_c, jnp.swapaxes(w_h, 1, 2)], axis=2)
    w2 = jnp.concatenate([x[:, 192:384], jnp.swapaxes(w_m, 1, 2)], axis=2)
    o = w_o.reshape(layers, 3, 3, 2, CH, CH).transpose(0, 1, 5, 3, 2, 4).reshape(layers, 192, 384)
    last = w_last.reshape(layers, 2, CH, CH).transpose(0, 3, 1, 2)
    mix = jnp.zeros((layers, CH, 2, 3, CH), BF).at[:, :, :, 1].set(last).reshape(layers, CH, 384)
    return w1, w2, jnp.concatenate([o, mix], axis=1)


def on_device(frames, hidden_in, cell_in, memory_in, w_x, w_h, w_m, w_o, w_last):
    core = lax.axis_index("layer")
    chip = lax.axis_index("rows")
    lower = core == 0
    chips = lax.axis_size("rows")
    swap = [(0, 1), (1, 0)]
    groups = [[4 * i + j for j in range(4)] for i in range(chips // 4)]
    across = []
    for i in range(chips):
        across.append((chips + i, (i + 4) % chips))
        across.append((i, chips + (i - 4) % chips))

    def to_partner(value):
        return lax.ppermute(value, "layer", swap)

    def to_neighbour(value):
        return lax.ppermute(value, ("layer", "rows"), across)

    own_w = prepare_weights(w_x, w_h, w_m, w_o, w_last)
    other_w = [to_partner(w) for w in own_w]
    w_low = [jnp.where(lower, a, b) for a, b in zip(own_w, other_w)]
    w_high = [jnp.where(lower, b, a) for a, b in zip(own_w, other_w)]

    extra = jnp.where(
        lower,
        jnp.stack([memory_in, frames[0]], axis=1),
        jnp.stack([frames[1], frames[2]], axis=1),
    )
    mine = jnp.concatenate(
        [hidden_in.transpose(1, 0, 2, 3, 4), cell_in.transpose(1, 0, 2, 3, 4), extra], axis=1
    )
    mine = lax.all_to_all(mine, "rows", 0, 0, axis_index_groups=groups, tiled=True)
    mine = mine.transpose(1, 0, 2, 3, 4).reshape(6, 8, CH, GW)
    theirs = to_partner(mine)
    low = jnp.where(lower, mine, theirs)
    high = jnp.where(lower, theirs, mine)
    low_own = lax.dynamic_slice_in_dim(low, 4 * core, OWN, axis=1)
    high_own = lax.dynamic_slice_in_dim(high, 4 * core, OWN, axis=1)
    low_partner = lax.dynamic_slice_in_dim(low, 4 * (1 - core), OWN, axis=1)
    high_partner = lax.dynamic_slice_in_dim(high, 4 * (1 - core), OWN, axis=1)

    def message(stack, order, layout, last_rows):
        parts = []
        for index, name in order:
            count = layout[name][1]
            parts.append(
                jnp.where(last_rows, stack[index, OWN - count :], stack[index, :count])
            )
        return jnp.concatenate(parts, axis=0)

    order_a = ((1, "HT"), (4, "M"), (0, "HB"), (2, "CB"), (3, "CT"), (5, "F0"))
    order_b = ((1, "HT"), (0, "HB"), (2, "CB"), (3, "CT"), (4, "F1"), (5, "F2"))
    upper = jnp.logical_not(lower)
    near_a = message(low_partner, order_a, FIRST_A, upper)
    near_b = message(high_partner, order_b, FIRST_B, upper)
    far_a = to_neighbour(message(low_own, order_a, FIRST_A, upper))
    far_b = to_neighbour(message(high_own, order_b, FIRST_B, upper))

    scalars = jnp.stack([core, 8 * (chip // 4) + 4 * core]).astype(jnp.int32)
    base = {"sc": scalars}
    low_state = ("low_state", low_own)
    high_state = ("high_state", high_own)
    halo_low = {k: ("na", "fa") + FIRST_A[k] for k in ("HB", "HT", "CB", "CT")}
    halo_high = {k: ("nb", "fb") + FIRST_B[k] for k in ("HB", "HT", "CB", "CT")}
    halo_m = ("na", "fa") + FIRST_A["M"]
    own_m = ("low0", 4)
    arrays = {"low0": low_own, "high0": high_own, "na": near_a, "fa": far_a, "nb": near_b, "fb": far_b}
    frame_field = (
        (("low0", 5), ("na", "fa") + FIRST_A["F0"]),
        (("high0", 4), ("nb", "fb") + FIRST_B["F1"]),
        (("high0", 5), ("nb", "fb") + FIRST_B["F2"]),
    )
    low_name, high_name = "low0", "high0"
    low_result = high_result = None
    for step in range(3):
        for half in range(2):
            last = step == 2 and half == 1
            tag = f"{step}{half}"
            state_name = high_name if half else low_name
            halo = halo_high if half else halo_low
            fields = {
                k: ((state_name, slot), halo[k])
                for slot, k in enumerate(("HB", "HT", "CB", "CT"))
            }
            fields["M"] = (own_m, halo_m)
            fields["X"] = x_field if half else frame_field[step]
            needed = {f[0][0] for f in fields.values()} | {n for f in fields.values() for n in f[1][:2]}
            operands = dict(base)
            for name in sorted(needed):
                operands[name] = arrays[name]
            for name, w in zip(("w1", "w2", "wo"), w_high if half else w_low):
                operands[name] = w
            outs = run_phase(operands, {"fields": fields}, last)
            state = outs[0]
            arrays["s" + tag] = state
            if half:
                high_name, high_result = "s" + tag, state
            else:
                low_name, low_result = "s" + tag, state
            own_m = ("s" + tag, 4)
            if not last:
                arrays["n" + tag] = to_partner(outs[1])
                arrays["f" + tag] = to_neighbour(outs[2])
                where = ("n" + tag, "f" + tag)
                halo_m = where + RUN["M"]
                new_halo = {k: where + RUN[k] for k in ("HB", "HT", "CB", "CT")}
                if half:
                    halo_high = new_halo
                else:
                    halo_low = new_halo
                    x_field = (("s" + tag, 1), where + RUN["HT"])

    keep = jnp.where(lower, low_result, high_result)
    give = jnp.where(lower, high_result, low_result)
    taken = to_partner(give)
    rows8 = jnp.concatenate(
        [jnp.where(lower, keep, taken), jnp.where(lower, taken, keep)], axis=1
    )
    by_chip = rows8.reshape(5, 4, 2, CH, GW).transpose(1, 0, 2, 3, 4)
    by_seq = lax.all_to_all(by_chip, "rows", 0, 0, axis_index_groups=groups, tiled=True)
    done = by_seq.transpose(1, 0, 2, 3, 4)
    return done[0:2], done[2:4], done[4:5]


def solution(mesh):
    return jax.shard_map(
        on_device,
        mesh=mesh,
        in_specs=(
            P(None, None, "rows", None, None),
            P("layer", None, "rows", None, None),
            P("layer", None, "rows", None, None),
            P(None, "rows", None, None),
            P("layer", None, None),
            P("layer", None, None),
            P("layer", None, None),
            P("layer", None, None),
            P("layer", None, None),
        ),
        out_specs=(
            P("layer", None, "rows", None, None),
            P("layer", None, "rows", None, None),
            P("layer", None, "rows", None, None),
        ),
        check_vma=False,
    )
```

```python
import functools

import jax
import jax.numpy as jnp
from jax import lax
from jax.experimental import pallas as pl
from jax.experimental.pallas import tpu as pltpu
from jax.sharding import PartitionSpec as P


CH = 64
GW = 128
OWN = 4
BF = jnp.bfloat16
F32 = jnp.float32

FIRST_A = {"HT": (0, 2), "M": (2, 4), "HB": (6, 4), "CB": (10, 3), "CT": (13, 1), "F0": (14, 4)}
FIRST_B = {"HT": (0, 2), "HB": (2, 4), "CB": (6, 3), "CT": (9, 1), "F1": (10, 4), "F2": (14, 4)}
SOON = ({"HT": (0, 4), "M": (4, 4)}, {"M": (0, 4)})
LATE = (
    {"HB": (0, 4), "CB": (4, 3), "CT": (7, 1)},
    {"HT": (0, 2), "HB": (2, 4), "CB": (6, 3), "CT": (9, 1)},
)
SLOT = {"HB": 0, "HT": 1, "CB": 2, "CT": 3, "M": 4}
REACH = (3, 1)


def units(layout):
    return sum(count for _, count in layout.values())


def both(half):
    shift = units(SOON[half])
    near = dict(SOON[half])
    near.update({k: (o + shift, n) for k, (o, n) in LATE[half].items()})
    return near


def sigmoid(v):
    return 0.5 * jnp.tanh(0.5 * v) + 0.5


def taps_of(row):
    lane = lax.broadcasted_iota(jnp.int32, row.shape, 1)
    zero = jnp.zeros_like(row)
    before = jnp.where(lane == 0, zero, pltpu.roll(row, 1, 1))
    after = jnp.where(lane == GW - 1, zero, pltpu.roll(row, GW - 1, 1))
    return jnp.concatenate([before, row, after], axis=0)


def phase_kernel(plan, *refs):
    names = plan["names"]
    outs = plan["outs"]
    n_in = len(names)
    ref = dict(zip(names, refs[:n_in]))
    out = dict(zip(outs, refs[n_in : n_in + len(outs)]))
    tx, th, tm, tx2, th2, tm2, yb, ob, yb2, ob2, raw = refs[n_in + len(outs) :]
    state_out = out["state"]
    core = ref["sc"][0]
    top = ref["sc"][1]
    first_core = core == 0

    def keep(row, value):
        if 0 <= row < OWN:
            return value
        g = top + row
        return jnp.where(jnp.logical_and(g >= 0, g < 128), value, jnp.zeros_like(value))

    def fetch(field, row):
        (own, slot), (near, near_at, far, far_at, count) = plan["fields"][field]
        if 0 <= row < OWN:
            return ref[own][slot, row]
        if row < 0:
            unit = count + row
            value = jnp.where(first_core, ref[far][far_at + unit], ref[near][near_at + unit])
        else:
            unit = row - OWN
            value = jnp.where(first_core, ref[near][near_at + unit], ref[far][far_at + unit])
        return keep(row, value)

    rows_of = [list(range(-reach, OWN + reach)) for reach in REACH]
    bufs = ((tx, th, tm, yb, ob), (tx2, th2, tm2.at[1:9], yb2, ob2))
    filled = set()

    def fill(buf, key, field, reach, upto):
        for i in range(upto):
            if (key, i) not in filled:
                filled.add((key, i))
                buf[i] = taps_of(fetch(field, i - reach))

    def matmuls(index, q):
        bx, bh, bm, _, _ = bufs[index]
        if index == 0:
            fill(tx, "x", "X", 4, q + 4)
            fill(th, "h", "HB", 4, q + 4)
            fill(tm, "m", "M", 4, q + 4)
        else:
            fill(th2, "h2", "HT", 2, q + 4)
        cols = [
            jnp.concatenate([buf[i + a] for buf in (bx, bh, bm) for a in range(3)], axis=0)
            for i in (q, q + 1)
        ]
        rhs = jnp.concatenate(cols, axis=1)
        x, h, m = rhs[0:576], rhs[576:1152], rhs[1152:1728]
        layer = plan["layer"] + index
        shared = jnp.dot(
            ref["wb"][layer],
            jnp.concatenate([x, h[512:576], m[0:128]], axis=0),
            preferred_element_type=F32,
        )
        slot = (q // 2 + index) % 2
        raw[slot, 0:256] = shared[0:256] + jnp.dot(
            ref["wa"][layer], h[0:512], preferred_element_type=F32
        )
        raw[slot, 256:448] = shared[256:448] + jnp.dot(
            ref["wc"][layer], m[128:576], preferred_element_type=F32
        )
        return raw.at[slot, 0:256], raw.at[slot, 256:448]

    def gates(index, q, acc1, acc2):
        _, _, _, y_buf, o_buf = bufs[index]
        rows = rows_of[index]
        pair = (rows[q], rows[q + 1])
        c_field = "CT" if index else "CB"
        c_prev = jnp.concatenate([fetch(c_field, row) for row in pair], axis=1).astype(F32)
        if index:
            m_rows = [tm2[row + 3, 64:128] for row in pair]
        else:
            m_rows = [tm[row + 4, 64:128] for row in pair]
        m_prev = jnp.concatenate(m_rows, axis=1).astype(F32)
        c_new = sigmoid(acc1[64:128] + 1.0) * c_prev + sigmoid(acc1[0:64]) * jnp.tanh(acc1[128:192])
        m_new = sigmoid(acc2[64:128] + 1.0) * m_prev + sigmoid(acc2[0:64]) * jnp.tanh(acc2[128:192])
        c_new = c_new.astype(BF)
        m_new = m_new.astype(BF)
        lanes = slice(q * GW, (q + 2) * GW)
        o_buf[:, lanes] = acc1[192:256]
        blocks = []
        for j, row in enumerate(pair):
            c_row = keep(row, c_new[:, j * GW : (j + 1) * GW])
            m_row = keep(row, m_new[:, j * GW : (j + 1) * GW])
            if 0 <= row < OWN:
                state_out[SLOT[c_field], row] = c_row
                if index:
                    state_out[SLOT["M"], row] = m_row
            c_taps = taps_of(c_row)
            m_taps = taps_of(m_row)
            if not index:
                tm2[row + 3] = m_taps
            blocks.append(
                jnp.concatenate(
                    [t[64 * b : 64 * b + 64] for b in range(3) for t in (c_taps, m_taps)], axis=0
                )
            )
        y_buf[:, lanes] = jnp.dot(
            ref["wo"][plan["layer"] + index],
            jnp.concatenate(blocks, axis=1),
            preferred_element_type=F32,
        )

    def hidden(index, q):
        _, _, _, y_buf, o_buf = bufs[index]
        lanes = slice(q * GW, (q + 1) * GW)
        gate = (
            o_buf[:, lanes]
            + y_buf[0:64, (q - 1) * GW : q * GW]
            + y_buf[64:128, lanes]
            + y_buf[128:192, (q + 1) * GW : (q + 2) * GW]
        )
        h_new = (sigmoid(gate) * jnp.tanh(y_buf[192:256, lanes])).astype(BF)
        row = rows_of[index][q]
        h_new = keep(row, h_new)
        if 0 <= row < OWN:
            state_out[SLOT["HT" if index else "HB"], row] = h_new
        if not index:
            tx2[row + 2] = taps_of(h_new)

    def finish(index, q, accs):
        gates(index, q, *accs)
        for h in (q - 1, q):
            if h >= 1:
                hidden(index, h)

    tasks = [(i, q) for i in range(2) for q in range(0, len(rows_of[i]), 2)]
    waiting = None
    for task in tasks:
        accs = matmuls(*task)
        if waiting is not None:
            finish(*waiting)
        waiting = task + (accs,)
    finish(*waiting)

    def send(target, layout, last_rows_if):
        for field, (offset, count) in layout.items():
            for u in range(count):
                low = state_out[SLOT[field], u]
                high = state_out[SLOT[field], OWN - count + u]
                target[offset + u] = jnp.where(last_rows_if, high, low)

    half = plan["half"]
    if "near" in out:
        send(out["near"], both(half) if "late" in out else SOON[half], first_core)
    if "soon" in out:
        send(out["soon"], SOON[half], jnp.logical_not(first_core))
    if "late" in out:
        send(out["late"], LATE[half], jnp.logical_not(first_core))


def run_phase(operands, plan):
    names = list(operands)
    plan = dict(plan, names=names)
    unit = (CH, GW)
    half = plan["half"]
    sizes = {"state": (5, OWN) + unit}
    if plan["send"]:
        far = {"soon": units(SOON[half])}
        if plan["send"] > 1:
            far["late"] = units(LATE[half])
        sizes["near"] = (sum(far.values()),) + unit
        sizes.update({k: (n,) + unit for k, n in far.items()})
    plan["outs"] = list(sizes)
    in_specs = [
        pl.BlockSpec(memory_space=pltpu.SMEM if name == "sc" else pltpu.VMEM) for name in names
    ]
    results = pl.pallas_call(
        functools.partial(phase_kernel, plan),
        out_shape=[jax.ShapeDtypeStruct(s, BF) for s in sizes.values()],
        in_specs=in_specs,
        out_specs=[pl.BlockSpec(memory_space=pltpu.VMEM) for _ in sizes],
        scratch_shapes=[
            pltpu.VMEM((12, 3 * CH, GW), BF),
            pltpu.VMEM((12, 3 * CH, GW), BF),
            pltpu.VMEM((12, 3 * CH, GW), BF),
            pltpu.VMEM((8, 3 * CH, GW), BF),
            pltpu.VMEM((8, 3 * CH, GW), BF),
            pltpu.VMEM((10, 3 * CH, GW), BF),
            pltpu.VMEM((4 * CH, 10 * GW), F32),
            pltpu.VMEM((CH, 10 * GW), F32),
            pltpu.VMEM((4 * CH, 6 * GW), F32),
            pltpu.VMEM((CH, 6 * GW), F32),
            pltpu.VMEM((2, 7 * CH, 2 * GW), F32),
        ],
        compiler_params=pltpu.CompilerParams(vmem_limit_bytes=24 << 20),
        name="two_layers",
    )(*[operands[name] for name in names])
    return dict(zip(sizes, results))


def pack_weights_kernel(sc, *refs):
    inputs, (wa, wb, wc, wo) = refs[:10], refs[10:]
    core = sc[0]
    for group in range(2):
        x, h, m, o, last = inputs[5 * group : 5 * group + 5]
        first = 2 * core if group == 0 else 2 - 2 * core
        for l in range(2):
            at = first + l
            xt = x[l]
            ht = jnp.transpose(h[l])
            mt = m[l]
            ot = o[l]
            wa[at] = ht[:, 0:512]
            wc[at] = mt[:, 128:576]
            gate_rows = jnp.concatenate([xt[0:192], xt[384:448]], axis=0)
            wb[at, 0:256, 0:512] = gate_rows[:, 0:512]
            wb[at, 0:256, 512:640] = jnp.concatenate([gate_rows[:, 512:576], ht[:, 512:576]], axis=1)
            wb[at, 0:256, 640:768] = jnp.zeros((256, 128), BF)
            wb[at, 256:448, 0:512] = xt[192:384, 0:512]
            wb[at, 256:448, 512:640] = jnp.concatenate(
                [xt[192:384, 512:576], jnp.zeros((192, 64), BF)], axis=1
            )
            wb[at, 256:448, 640:768] = mt[:, 0:128]
            for a in range(3):
                wo[at, 64 * a : 64 * a + 64] = ot[:, 384 * a : 384 * a + 384]
            wo[at, 192:256, 0:128] = jnp.zeros((64, 128), BF)
            wo[at, 192:256, 128:256] = last[l]
            wo[at, 192:256, 256:384] = jnp.zeros((64, 128), BF)


def pack_weights(scalars, own, other):
    shapes = ((4, 256, 512), (4, 448, 768), (4, 192, 448), (4, 256, 384))
    vmem = pl.BlockSpec(memory_space=pltpu.VMEM)
    return pl.pallas_call(
        pack_weights_kernel,
        out_shape=[jax.ShapeDtypeStruct(s, BF) for s in shapes],
        in_specs=[pl.BlockSpec(memory_space=pltpu.SMEM)] + [vmem] * 10,
        out_specs=[vmem] * 4,
        compiler_params=pltpu.CompilerParams(vmem_limit_bytes=32 << 20),
        name="pack_weights",
    )(scalars, *own, *other)


def cut_state_kernel(sc, frames, hidden, cell, memory, *rest):
    pieces, sems = rest[:4], rest[4]
    core, z = sc[0], sc[2]
    shared = []
    for k in range(4):
        seq = lax.rem(z + k, 4)
        for l in range(2):
            shared.append(
                pltpu.make_async_copy(hidden.at[l, seq], pieces[k].at[l], sems.at[k, l])
            )
            shared.append(
                pltpu.make_async_copy(cell.at[l, seq], pieces[k].at[2 + l], sems.at[k, 2 + l])
            )
    for c in shared:
        c.start()

    def extras(sources):
        copies = []
        for k in range(4):
            seq = lax.rem(z + k, 4)
            for i, source in enumerate(sources(seq)):
                copies.append(
                    pltpu.make_async_copy(source, pieces[k].at[4 + i], sems.at[k, 4 + i])
                )
        for c in copies:
            c.start()
        for c in copies:
            c.wait()

    @pl.when(core == 0)
    def _():
        extras(lambda seq: (memory.at[seq], frames.at[0, seq]))

    @pl.when(core != 0)
    def _():
        extras(lambda seq: (frames.at[1, seq], frames.at[2, seq]))

    for c in shared:
        c.wait()


def cut_state(scalars, frames, hidden, cell, memory):
    anywhere = pl.BlockSpec(memory_space=pl.ANY)
    return pl.pallas_call(
        cut_state_kernel,
        out_shape=[jax.ShapeDtypeStruct((6, 2, CH, GW), BF)] * 4,
        in_specs=[pl.BlockSpec(memory_space=pltpu.SMEM)] + [anywhere] * 4,
        out_specs=[anywhere] * 4,
        scratch_shapes=[pltpu.SemaphoreType.DMA((4, 6))],
        name="cut_state",
    )(scalars, frames, hidden, cell, memory)


ORDER_A = ((1, "HT"), (4, "M"), (0, "HB"), (2, "CB"), (3, "CT"), (5, "F0"))
ORDER_B = ((1, "HT"), (0, "HB"), (2, "CB"), (3, "CT"), (4, "F1"), (5, "F2"))


def open_state_kernel(sc, *refs):
    mine, theirs = refs[:4], refs[4:8]
    low_own, high_own, near_a, near_b, far_a, far_b, rows = refs[8:]
    core, z = sc[0], sc[2]
    for k in range(4):
        at = 2 * lax.rem(z + 4 - k, 4)
        for i in range(2):
            for a in range(6):
                rows[0, a, at + i] = mine[k][a, i]
                rows[1, a, at + i] = theirs[k][a, i]
    other = 1 - core
    for a in range(6):
        for r in range(OWN):
            low_own[a, r] = rows[core, a, 4 * core + r]
            high_own[a, r] = rows[other, a, 4 * core + r]
    for group, order, layout, near, far in (
        (core, ORDER_A, FIRST_A, near_a, far_a),
        (other, ORDER_B, FIRST_B, near_b, far_b),
    ):
        for a, name in order:
            offset, count = layout[name]
            for u in range(count):
                turn = core * (OWN - count) + u
                far[offset + u] = rows[group, a, 4 * core + turn]
                near[offset + u] = rows[group, a, 4 * other + turn]


def open_state(scalars, mine, theirs):
    vmem = pl.BlockSpec(memory_space=pltpu.VMEM)
    shapes = [(6, OWN)] * 2 + [(18,)] * 4
    return pl.pallas_call(
        open_state_kernel,
        out_shape=[jax.ShapeDtypeStruct(s + (CH, GW), BF) for s in shapes],
        in_specs=[pl.BlockSpec(memory_space=pltpu.SMEM)] + [vmem] * 8,
        out_specs=[vmem] * 6,
        scratch_shapes=[pltpu.VMEM((2, 6, 8, CH, GW), BF)],
        compiler_params=pltpu.CompilerParams(vmem_limit_bytes=16 << 20),
        name="open_state",
    )(scalars, *mine, *theirs)


def cut_result_kernel(sc, own, taken, *pieces):
    core, z = sc[0], sc[2]
    for k in range(4):
        to = lax.rem(z + k, 4)
        here = (to // 2) == core
        row = 2 * lax.rem(to, 2)
        for a in range(5):
            for i in range(2):
                pieces[k][a, i] = jnp.where(here, own[a, row + i], taken[a, row + i])


def cut_result(scalars, own, taken):
    vmem = pl.BlockSpec(memory_space=pltpu.VMEM)
    return pl.pallas_call(
        cut_result_kernel,
        out_shape=[jax.ShapeDtypeStruct((5, 2, CH, GW), BF)] * 4,
        in_specs=[pl.BlockSpec(memory_space=pltpu.SMEM), vmem, vmem],
        out_specs=[vmem] * 4,
        compiler_params=pltpu.CompilerParams(vmem_limit_bytes=8 << 20),
        name="cut_result",
    )(scalars, own, taken)


def close_result_kernel(sc, *refs):
    low, high = refs[:4], refs[4:8]
    hidden, cell, memory = refs[8:]
    core, z = sc[0], sc[2]
    for k in range(4):
        seq = lax.rem(z + 4 - k, 4)
        for i in range(2):
            for a in range(5):
                value = jnp.where(core == 0, low[k][a, i], high[k][a, i])
                if a < 2:
                    hidden[a, seq, i] = value
                elif a < 4:
                    cell[a - 2, seq, i] = value
                else:
                    memory[0, seq, i] = value


def close_result(scalars, low, high):
    vmem = pl.BlockSpec(memory_space=pltpu.VMEM)
    shapes = ((2, 4, 2), (2, 4, 2), (1, 4, 2))
    return pl.pallas_call(
        close_result_kernel,
        out_shape=[jax.ShapeDtypeStruct(s + (CH, GW), BF) for s in shapes],
        in_specs=[pl.BlockSpec(memory_space=pltpu.SMEM)] + [vmem] * 8,
        out_specs=[vmem] * 3,
        compiler_params=pltpu.CompilerParams(vmem_limit_bytes=8 << 20),
        name="close_result",
    )(scalars, *low, *high)


def program(frames, hidden_in, cell_in, memory_in, w_x, w_h, w_m, w_o, w_last):
    core = lax.axis_index("layer")
    chip = lax.axis_index("rows")
    chips = lax.axis_size("rows")
    swap = [(0, 1), (1, 0)]
    across = []
    for i in range(chips):
        across.append((chips + i, (i + 4) % chips))
        across.append((i, chips + (i - 4) % chips))

    def to_partner(value):
        return lax.ppermute(value, "layer", swap)

    def to_neighbour(value):
        return lax.ppermute(value, ("layer", "rows"), across)

    def around(value, k, cores=None):
        turn = [(i, 4 * (i // 4) + (i + k) % 4) for i in range(chips)]
        if cores is None:
            return lax.ppermute(value, "rows", turn)
        pairs = [(cores * chips + i, cores * chips + j) for i, j in turn]
        return lax.ppermute(value, ("layer", "rows"), pairs)

    scalars = jnp.stack([core, 8 * (chip // 4) + 4 * core, chip % 4]).astype(jnp.int32)
    turned = [jnp.swapaxes(w, 1, 2) for w in (w_x, w_m, w_o, w_last)]
    own_w = [turned[0], w_h, turned[1], turned[2], turned[3]]
    other_w = [to_partner(w) for w in own_w]
    wa, wb, wc, wo = pack_weights(scalars, own_w, other_w)

    pieces = cut_state(scalars, frames, hidden_in, cell_in, memory_in)
    mine = [pieces[0]] + [around(pieces[k], k) for k in (1, 2, 3)]
    theirs = [to_partner(piece) for piece in mine]
    low_own, high_own, near_a, near_b, message_a, message_b = open_state(scalars, mine, theirs)
    far_a = to_neighbour(message_a)
    far_b = to_neighbour(message_b)

    base = {"sc": scalars, "wa": wa, "wb": wb, "wc": wc, "wo": wo}
    arrays = {"s00": low_own, "s01": high_own, "na": near_a, "fa": far_a, "nb": near_b, "fb": far_b}

    def first(letter, layout, field):
        offset, count = layout[field]
        return ("n" + letter, offset, "f" + letter, offset, count)

    kept = ("HB", "HT", "CB", "CT")
    halo = [{k: first("a", FIRST_A, k) for k in kept}, {k: first("b", FIRST_B, k) for k in kept}]
    states = ["s00", "s01"]
    own_m = ("s00", 4)
    halo_m = first("a", FIRST_A, "M")
    frame_field = (
        (("s00", 5), first("a", FIRST_A, "F0")),
        (("s01", 4), first("b", FIRST_B, "F1")),
        (("s01", 5), first("b", FIRST_B, "F2")),
    )
    steps = frames.shape[0]
    results = [None, None]
    for step in range(steps):
        x_field = frame_field[step]
        for half in range(2):
            send = 2 if step < steps - 1 else 1 - half
            fields = {k: ((states[half], SLOT[k]), halo[half][k]) for k in kept}
            fields["M"] = (own_m, halo_m)
            fields["X"] = x_field
            needed = {f[0][0] for f in fields.values()}
            needed |= {f[1][i] for f in fields.values() for i in (0, 2)}
            operands = dict(base)
            for name in sorted(needed):
                operands[name] = arrays[name]
            plan = {"fields": fields, "half": half, "layer": 2 * half, "send": send}
            tag = f"{step}{half}"
            outs = run_phase(operands, plan)
            results[half] = outs["state"]
            states[half] = "state" + tag
            arrays["state" + tag] = outs["state"]
            own_m = ("state" + tag, SLOT["M"])
            if send:
                arrays["soon" + tag] = to_neighbour(outs["soon"])
                arrays["near" + tag] = to_partner(outs["near"])
                near_at = both(half)
                for k, (o, n) in SOON[half].items():
                    spec = ("near" + tag, near_at[k][0], "soon" + tag, o, n)
                    if k == "M":
                        halo_m = spec
                    else:
                        x_field = (("state" + tag, SLOT["HT"]), spec)
                        halo[half][k] = spec
            if send > 1:
                arrays["late" + tag] = to_neighbour(outs["late"])
                for k, (o, n) in LATE[half].items():
                    halo[half][k] = ("near" + tag, near_at[k][0], "late" + tag, o, n)

    done = []
    for half in range(2):
        taken = lax.ppermute(results[half], "layer", [(1 - half, half)])
        pieces = cut_result(scalars, results[half], taken)
        done.append([pieces[0]] + [around(pieces[k], k, half) for k in (1, 2, 3)])
    return tuple(close_result(scalars, *done))


def solution(mesh):
    return jax.shard_map(
        program,
        mesh=mesh,
        in_specs=(
            P(None, None, "rows", None, None),
            P("layer", None, "rows", None, None),
            P("layer", None, "rows", None, None),
            P(None, "rows", None, None),
            P("layer", None, None),
            P("layer", None, None),
            P("layer", None, None),
            P("layer", None, None),
            P("layer", None, None),
        ),
        out_specs=(
            P("layer", None, "rows", None, None),
            P("layer", None, "rows", None, None),
            P("layer", None, "rows", None, None),
        ),
        check_vma=False,
    )
```

```python
import functools

import jax
import jax.numpy as jnp
from jax import lax
from jax.experimental import pallas as pl
from jax.experimental.pallas import tpu as pltpu
from jax.sharding import PartitionSpec as P


CH = 64
GW = 128
OWN = 4
BF = jnp.bfloat16
F32 = jnp.float32

FIRST_A = {"HT": (0, 2), "M": (2, 4), "HB": (6, 4), "CB": (10, 3), "CT": (13, 1), "F0": (14, 4)}
FIRST_B = {"HT": (0, 2), "HB": (2, 4), "CB": (6, 3), "CT": (9, 1), "F1": (10, 4), "F2": (14, 4)}
SOON = ({"HT": (0, 4), "M": (4, 4)}, {"M": (0, 4)})
LATE = (
    {"HB": (0, 4), "CB": (4, 3), "CT": (7, 1)},
    {"HT": (0, 2), "HB": (2, 4), "CB": (6, 3), "CT": (9, 1)},
)
SLOT = {"HB": 0, "HT": 1, "CB": 2, "CT": 3, "M": 4}
REACH = (3, 1)


def units(layout):
    return sum(count for _, count in layout.values())


def both(half):
    shift = units(SOON[half])
    near = dict(SOON[half])
    near.update({k: (o + shift, n) for k, (o, n) in LATE[half].items()})
    return near


def sigmoid(v):
    return 0.5 * jnp.tanh(0.5 * v) + 0.5


def taps_of(row):
    lane = lax.broadcasted_iota(jnp.int32, row.shape, 1)
    zero = jnp.zeros_like(row)
    before = jnp.where(lane == 0, zero, pltpu.roll(row, 1, 1))
    after = jnp.where(lane == GW - 1, zero, pltpu.roll(row, GW - 1, 1))
    return jnp.concatenate([before, row, after], axis=0)


def phase_kernel(plan, *refs):
    names = plan["names"]
    outs = plan["outs"]
    n_in = len(names)
    ref = dict(zip(names, refs[:n_in]))
    out = dict(zip(outs, refs[n_in : n_in + len(outs)]))
    tx, th, tm, tx2, th2, tm2, yb, ob, yb2, ob2, raw = refs[n_in + len(outs) :]
    state_out = out["state"]
    core = ref["sc"][0]
    top = ref["sc"][1]
    first_core = core == 0

    def keep(row, value):
        if 0 <= row < OWN:
            return value
        g = top + row
        return jnp.where(jnp.logical_and(g >= 0, g < 128), value, jnp.zeros_like(value))

    def fetch(field, row):
        (own, slot), (near, near_at, far, far_at, count) = plan["fields"][field]
        if 0 <= row < OWN:
            return ref[own][slot, row]
        if row < 0:
            unit = count + row
            value = jnp.where(first_core, ref[far][far_at + unit], ref[near][near_at + unit])
        else:
            unit = row - OWN
            value = jnp.where(first_core, ref[near][near_at + unit], ref[far][far_at + unit])
        return keep(row, value)

    rows_of = [list(range(-reach, OWN + reach)) for reach in REACH]
    bufs = ((tx, th, tm, yb, ob), (tx2, th2, tm2.at[1:9], yb2, ob2))
    filled = set()

    def fill(buf, key, field, reach, upto):
        for i in range(upto):
            if (key, i) not in filled:
                filled.add((key, i))
                buf[i] = taps_of(fetch(field, i - reach))

    def matmuls(index, q):
        bx, bh, bm, _, _ = bufs[index]
        if index == 0:
            fill(tx, "x", "X", 4, q + 4)
            fill(th, "h", "HB", 4, q + 4)
            fill(tm, "m", "M", 4, q + 4)
        else:
            fill(th2, "h2", "HT", 2, q + 4)
        cols = [
            jnp.concatenate([buf[i + a] for buf in (bx, bh, bm) for a in range(3)], axis=0)
            for i in (q, q + 1)
        ]
        rhs = jnp.concatenate(cols, axis=1)
        x, h, m = rhs[0:576], rhs[576:1152], rhs[1152:1728]
        layer = plan["layer"] + index
        shared = jnp.dot(
            ref["wb"][layer],
            jnp.concatenate([x, h[512:576], m[0:128]], axis=0),
            preferred_element_type=F32,
        )
        slot = (q // 2 + index) % 2
        raw[slot, 0:256] = shared[0:256] + jnp.dot(
            ref["wa"][layer], h[0:512], preferred_element_type=F32
        )
        raw[slot, 256:448] = shared[256:448] + jnp.dot(
            ref["wc"][layer], m[128:576], preferred_element_type=F32
        )
        return raw.at[slot, 0:256], raw.at[slot, 256:448]

    def gates(index, q, acc1, acc2):
        _, _, _, y_buf, o_buf = bufs[index]
        rows = rows_of[index]
        pair = (rows[q], rows[q + 1])
        c_field = "CT" if index else "CB"
        c_prev = jnp.concatenate([fetch(c_field, row) for row in pair], axis=1).astype(F32)
        if index:
            m_rows = [tm2[row + 3, 64:128] for row in pair]
        else:
            m_rows = [tm[row + 4, 64:128] for row in pair]
        m_prev = jnp.concatenate(m_rows, axis=1).astype(F32)
        c_new = sigmoid(acc1[64:128] + 1.0) * c_prev + sigmoid(acc1[0:64]) * jnp.tanh(acc1[128:192])
        m_new = sigmoid(acc2[64:128] + 1.0) * m_prev + sigmoid(acc2[0:64]) * jnp.tanh(acc2[128:192])
        c_new = c_new.astype(BF)
        m_new = m_new.astype(BF)
        lanes = slice(q * GW, (q + 2) * GW)
        o_buf[:, lanes] = acc1[192:256]
        blocks = []
        for j, row in enumerate(pair):
            c_row = keep(row, c_new[:, j * GW : (j + 1) * GW])
            m_row = keep(row, m_new[:, j * GW : (j + 1) * GW])
            if 0 <= row < OWN:
                state_out[SLOT[c_field], row] = c_row
                if index:
                    state_out[SLOT["M"], row] = m_row
            c_taps = taps_of(c_row)
            m_taps = taps_of(m_row)
            if not index:
                tm2[row + 3] = m_taps
            blocks.append(
                jnp.concatenate(
                    [t[64 * b : 64 * b + 64] for b in range(3) for t in (c_taps, m_taps)], axis=0
                )
            )
        y_buf[:, lanes] = jnp.dot(
            ref["wo"][plan["layer"] + index],
            jnp.concatenate(blocks, axis=1),
            preferred_element_type=F32,
        )

    def hidden(index, q):
        _, _, _, y_buf, o_buf = bufs[index]
        lanes = slice(q * GW, (q + 1) * GW)
        gate = (
            o_buf[:, lanes]
            + y_buf[0:64, (q - 1) * GW : q * GW]
            + y_buf[64:128, lanes]
            + y_buf[128:192, (q + 1) * GW : (q + 2) * GW]
        )
        h_new = (sigmoid(gate) * jnp.tanh(y_buf[192:256, lanes])).astype(BF)
        row = rows_of[index][q]
        h_new = keep(row, h_new)
        if 0 <= row < OWN:
            state_out[SLOT["HT" if index else "HB"], row] = h_new
        if not index:
            tx2[row + 2] = taps_of(h_new)

    def finish(index, q, accs):
        gates(index, q, *accs)
        for h in (q - 1, q):
            if h >= 1:
                hidden(index, h)

    tasks = [(i, q) for i in range(2) for q in range(0, len(rows_of[i]), 2)]
    waiting = None
    for task in tasks:
        accs = matmuls(*task)
        if waiting is not None:
            finish(*waiting)
        waiting = task + (accs,)
    finish(*waiting)

    def send(target, layout, last_rows_if):
        for field, (offset, count) in layout.items():
            for u in range(count):
                low = state_out[SLOT[field], u]
                high = state_out[SLOT[field], OWN - count + u]
                target[offset + u] = jnp.where(last_rows_if, high, low)

    half = plan["half"]
    if "near" in out:
        send(out["near"], both(half) if "late" in out else SOON[half], first_core)
    if "soon" in out:
        send(out["soon"], SOON[half], jnp.logical_not(first_core))
    if "late" in out:
        send(out["late"], LATE[half], jnp.logical_not(first_core))


def run_phase(operands, plan):
    names = list(operands)
    plan = dict(plan, names=names)
    unit = (CH, GW)
    half = plan["half"]
    sizes = {"state": (5, OWN) + unit}
    if plan["send"]:
        far = {"soon": units(SOON[half])}
        if plan["send"] > 1:
            far["late"] = units(LATE[half])
        sizes["near"] = (sum(far.values()),) + unit
        sizes.update({k: (n,) + unit for k, n in far.items()})
    plan["outs"] = list(sizes)
    in_specs = [
        pl.BlockSpec(memory_space=pltpu.SMEM if name == "sc" else pltpu.VMEM) for name in names
    ]
    results = pl.pallas_call(
        functools.partial(phase_kernel, plan),
        out_shape=[jax.ShapeDtypeStruct(s, BF) for s in sizes.values()],
        in_specs=in_specs,
        out_specs=[pl.BlockSpec(memory_space=pltpu.VMEM) for _ in sizes],
        scratch_shapes=[
            pltpu.VMEM((12, 3 * CH, GW), BF),
            pltpu.VMEM((12, 3 * CH, GW), BF),
            pltpu.VMEM((12, 3 * CH, GW), BF),
            pltpu.VMEM((8, 3 * CH, GW), BF),
            pltpu.VMEM((8, 3 * CH, GW), BF),
            pltpu.VMEM((10, 3 * CH, GW), BF),
            pltpu.VMEM((4 * CH, 10 * GW), F32),
            pltpu.VMEM((CH, 10 * GW), F32),
            pltpu.VMEM((4 * CH, 6 * GW), F32),
            pltpu.VMEM((CH, 6 * GW), F32),
            pltpu.VMEM((2, 7 * CH, 2 * GW), F32),
        ],
        compiler_params=pltpu.CompilerParams(vmem_limit_bytes=24 << 20),
        name="two_layers",
    )(*[operands[name] for name in names])
    return dict(zip(sizes, results))


def pack_weights_kernel(sc, *refs):
    inputs, (wa, wb, wc, wo) = refs[:10], refs[10:]
    core = sc[0]
    for group in range(2):
        x, h, m, o, last = inputs[5 * group : 5 * group + 5]
        first = 2 * core if group == 0 else 2 - 2 * core
        for l in range(2):
            at = first + l
            xt = x[l]
            ht = jnp.transpose(h[l])
            mt = m[l]
            ot = o[l]
            wa[at] = ht[:, 0:512]
            wc[at] = mt[:, 128:576]
            gate_rows = jnp.concatenate([xt[0:192], xt[384:448]], axis=0)
            wb[at, 0:256, 0:512] = gate_rows[:, 0:512]
            wb[at, 0:256, 512:640] = jnp.concatenate([gate_rows[:, 512:576], ht[:, 512:576]], axis=1)
            wb[at, 0:256, 640:768] = jnp.zeros((256, 128), BF)
            wb[at, 256:448, 0:512] = xt[192:384, 0:512]
            wb[at, 256:448, 512:640] = jnp.concatenate(
                [xt[192:384, 512:576], jnp.zeros((192, 64), BF)], axis=1
            )
            wb[at, 256:448, 640:768] = mt[:, 0:128]
            for a in range(3):
                wo[at, 64 * a : 64 * a + 64] = ot[:, 384 * a : 384 * a + 384]
            wo[at, 192:256, 0:128] = jnp.zeros((64, 128), BF)
            wo[at, 192:256, 128:256] = last[l]
            wo[at, 192:256, 256:384] = jnp.zeros((64, 128), BF)


def pack_weights(scalars, own, other):
    shapes = ((4, 256, 512), (4, 448, 768), (4, 192, 448), (4, 256, 384))
    vmem = pl.BlockSpec(memory_space=pltpu.VMEM)
    return pl.pallas_call(
        pack_weights_kernel,
        out_shape=[jax.ShapeDtypeStruct(s, BF) for s in shapes],
        in_specs=[pl.BlockSpec(memory_space=pltpu.SMEM)] + [vmem] * 10,
        out_specs=[vmem] * 4,
        compiler_params=pltpu.CompilerParams(vmem_limit_bytes=32 << 20),
        name="pack_weights",
    )(scalars, *own, *other)


def cut_state_kernel(sc, frames, hidden, cell, memory, *pieces):
    first_core, z = sc[0] == 0, sc[2]
    for k in range(4):
        seq = lax.rem(z + k, 4)
        for i in range(2):
            for l in range(2):
                pieces[k][l, i] = hidden[l, seq, i]
                pieces[k][2 + l, i] = cell[l, seq, i]
            pieces[k][4, i] = jnp.where(first_core, memory[seq, i], frames[1, seq, i])
            pieces[k][5, i] = jnp.where(first_core, frames[0, seq, i], frames[2, seq, i])


def cut_state(scalars, frames, hidden, cell, memory):
    vmem = pl.BlockSpec(memory_space=pltpu.VMEM)
    return pl.pallas_call(
        cut_state_kernel,
        out_shape=[jax.ShapeDtypeStruct((6, 2, CH, GW), BF)] * 4,
        in_specs=[pl.BlockSpec(memory_space=pltpu.SMEM)] + [vmem] * 4,
        out_specs=[vmem] * 4,
        compiler_params=pltpu.CompilerParams(vmem_limit_bytes=8 << 20),
        name="cut_state",
    )(scalars, frames, hidden, cell, memory)


ORDER_A = ((1, "HT"), (4, "M"), (0, "HB"), (2, "CB"), (3, "CT"), (5, "F0"))
ORDER_B = ((1, "HT"), (0, "HB"), (2, "CB"), (3, "CT"), (4, "F1"), (5, "F2"))


def open_state_kernel(sc, *refs):
    mine, theirs = refs[:4], refs[4:8]
    low_own, high_own, near_a, near_b, far_a, far_b, rows = refs[8:]
    core, z = sc[0], sc[2]
    for k in range(4):
        at = 2 * lax.rem(z + 4 - k, 4)
        for i in range(2):
            for a in range(6):
                rows[0, a, at + i] = mine[k][a, i]
                rows[1, a, at + i] = theirs[k][a, i]
    other = 1 - core
    for a in range(6):
        for r in range(OWN):
            low_own[a, r] = rows[core, a, 4 * core + r]
            high_own[a, r] = rows[other, a, 4 * core + r]
    for group, order, layout, near, far in (
        (core, ORDER_A, FIRST_A, near_a, far_a),
        (other, ORDER_B, FIRST_B, near_b, far_b),
    ):
        for a, name in order:
            offset, count = layout[name]
            for u in range(count):
                turn = core * (OWN - count) + u
                far[offset + u] = rows[group, a, 4 * core + turn]
                near[offset + u] = rows[group, a, 4 * other + turn]


def open_state(scalars, mine, theirs):
    vmem = pl.BlockSpec(memory_space=pltpu.VMEM)
    shapes = [(6, OWN)] * 2 + [(18,)] * 4
    return pl.pallas_call(
        open_state_kernel,
        out_shape=[jax.ShapeDtypeStruct(s + (CH, GW), BF) for s in shapes],
        in_specs=[pl.BlockSpec(memory_space=pltpu.SMEM)] + [vmem] * 8,
        out_specs=[vmem] * 6,
        scratch_shapes=[pltpu.VMEM((2, 6, 8, CH, GW), BF)],
        compiler_params=pltpu.CompilerParams(vmem_limit_bytes=16 << 20),
        name="open_state",
    )(scalars, *mine, *theirs)


def cut_result_kernel(sc, low, high, taken, *pieces):
    core, z = sc[0], sc[2]
    for k in range(4):
        to = lax.rem(z + k, 4)
        here = (to // 2) == core
        row = 2 * lax.rem(to, 2)
        for a in range(5):
            for i in range(2):
                own = jnp.where(core == 0, low[a, row + i], high[a, row + i])
                pieces[k][a, i] = jnp.where(here, own, taken[a, row + i])


def cut_result(scalars, low, high, taken):
    vmem = pl.BlockSpec(memory_space=pltpu.VMEM)
    return pl.pallas_call(
        cut_result_kernel,
        out_shape=[jax.ShapeDtypeStruct((5, 2, CH, GW), BF)] * 4,
        in_specs=[pl.BlockSpec(memory_space=pltpu.SMEM)] + [vmem] * 3,
        out_specs=[vmem] * 4,
        compiler_params=pltpu.CompilerParams(vmem_limit_bytes=8 << 20),
        name="cut_result",
    )(scalars, low, high, taken)


def close_result_kernel(sc, *refs):
    parts = refs[:4]
    hidden, cell, memory = refs[4:]
    z = sc[2]
    for k in range(4):
        seq = lax.rem(z + 4 - k, 4)
        for i in range(2):
            for a in range(2):
                hidden[a, seq, i] = parts[k][a, i]
                cell[a, seq, i] = parts[k][2 + a, i]
            memory[0, seq, i] = parts[k][4, i]


def close_result(scalars, parts):
    vmem = pl.BlockSpec(memory_space=pltpu.VMEM)
    shapes = ((2, 4, 2), (2, 4, 2), (1, 4, 2))
    return pl.pallas_call(
        close_result_kernel,
        out_shape=[jax.ShapeDtypeStruct(s + (CH, GW), BF) for s in shapes],
        in_specs=[pl.BlockSpec(memory_space=pltpu.SMEM)] + [vmem] * 4,
        out_specs=[vmem] * 3,
        compiler_params=pltpu.CompilerParams(vmem_limit_bytes=8 << 20),
        name="close_result",
    )(scalars, *parts)


def program(frames, hidden_in, cell_in, memory_in, w_x, w_h, w_m, w_o, w_last):
    core = lax.axis_index("layer")
    chip = lax.axis_index("rows")
    chips = lax.axis_size("rows")
    swap = [(0, 1), (1, 0)]
    across = []
    for i in range(chips):
        across.append((chips + i, (i + 4) % chips))
        across.append((i, chips + (i - 4) % chips))

    def to_partner(value):
        return lax.ppermute(value, "layer", swap)

    def to_neighbour(value):
        return lax.ppermute(value, ("layer", "rows"), across)

    def around(value, k):
        turn = [(i, 4 * (i // 4) + (i + k) % 4) for i in range(chips)]
        return lax.ppermute(value, "rows", turn)

    scalars = jnp.stack([core, 8 * (chip // 4) + 4 * core, chip % 4]).astype(jnp.int32)
    turned = [jnp.swapaxes(w, 1, 2) for w in (w_x, w_m, w_o, w_last)]
    own_w = [turned[0], w_h, turned[1], turned[2], turned[3]]
    other_w = [to_partner(w) for w in own_w]
    wa, wb, wc, wo = pack_weights(scalars, own_w, other_w)

    pieces = cut_state(scalars, frames, hidden_in, cell_in, memory_in)
    mine = [pieces[0]] + [around(pieces[k], k) for k in (1, 2, 3)]
    theirs = [to_partner(piece) for piece in mine]
    low_own, high_own, near_a, near_b, message_a, message_b = open_state(scalars, mine, theirs)
    far_a = to_neighbour(message_a)
    far_b = to_neighbour(message_b)

    base = {"sc": scalars, "wa": wa, "wb": wb, "wc": wc, "wo": wo}
    arrays = {"s00": low_own, "s01": high_own, "na": near_a, "fa": far_a, "nb": near_b, "fb": far_b}

    def first(letter, layout, field):
        offset, count = layout[field]
        return ("n" + letter, offset, "f" + letter, offset, count)

    kept = ("HB", "HT", "CB", "CT")
    halo = [{k: first("a", FIRST_A, k) for k in kept}, {k: first("b", FIRST_B, k) for k in kept}]
    states = ["s00", "s01"]
    own_m = ("s00", 4)
    halo_m = first("a", FIRST_A, "M")
    frame_field = (
        (("s00", 5), first("a", FIRST_A, "F0")),
        (("s01", 4), first("b", FIRST_B, "F1")),
        (("s01", 5), first("b", FIRST_B, "F2")),
    )
    steps = frames.shape[0]
    results = [None, None]
    for step in range(steps):
        x_field = frame_field[step]
        for half in range(2):
            send = 2 if step < steps - 1 else 1 - half
            fields = {k: ((states[half], SLOT[k]), halo[half][k]) for k in kept}
            fields["M"] = (own_m, halo_m)
            fields["X"] = x_field
            needed = {f[0][0] for f in fields.values()}
            needed |= {f[1][i] for f in fields.values() for i in (0, 2)}
            operands = dict(base)
            for name in sorted(needed):
                operands[name] = arrays[name]
            plan = {"fields": fields, "half": half, "layer": 2 * half, "send": send}
            tag = f"{step}{half}"
            outs = run_phase(operands, plan)
            results[half] = outs["state"]
            states[half] = "state" + tag
            arrays["state" + tag] = outs["state"]
            own_m = ("state" + tag, SLOT["M"])
            if send:
                arrays["soon" + tag] = to_neighbour(outs["soon"])
                arrays["near" + tag] = to_partner(outs["near"])
                near_at = both(half)
                for k, (o, n) in SOON[half].items():
                    spec = ("near" + tag, near_at[k][0], "soon" + tag, o, n)
                    if k == "M":
                        halo_m = spec
                    else:
                        x_field = (("state" + tag, SLOT["HT"]), spec)
                        halo[half][k] = spec
            if send > 1:
                arrays["late" + tag] = to_neighbour(outs["late"])
                for k, (o, n) in LATE[half].items():
                    halo[half][k] = ("near" + tag, near_at[k][0], "late" + tag, o, n)

    give = jnp.where(core == 0, results[1], results[0])
    taken = to_partner(give)
    pieces = cut_result(scalars, results[0], results[1], taken)
    done = [pieces[0]] + [around(pieces[k], k) for k in (1, 2, 3)]
    return tuple(close_result(scalars, done))


def solution(mesh):
    return jax.shard_map(
        program,
        mesh=mesh,
        in_specs=(
            P(None, None, "rows", None, None),
            P("layer", None, "rows", None, None),
            P("layer", None, "rows", None, None),
            P(None, "rows", None, None),
            P("layer", None, None),
            P("layer", None, None),
            P("layer", None, None),
            P("layer", None, None),
            P("layer", None, None),
        ),
        out_specs=(
            P("layer", None, "rows", None, None),
            P("layer", None, "rows", None, None),
            P("layer", None, "rows", None, None),
        ),
        check_vma=False,
    )
```

```python
import functools

import jax
import jax.numpy as jnp
from jax import lax
from jax.experimental import pallas as pl
from jax.experimental.pallas import tpu as pltpu
from jax.sharding import PartitionSpec as P


CH = 64
GW = 128
OWN = 4
BF = jnp.bfloat16
F32 = jnp.float32

FIRST_A = {"HT": (0, 2), "M": (2, 4), "HB": (6, 4), "CB": (10, 3), "CT": (13, 1), "F0": (14, 4)}
FIRST_B = {"HT": (0, 2), "HB": (2, 4), "CB": (6, 3), "CT": (9, 1), "F1": (10, 4), "F2": (14, 4)}
SOON = ({"HT": (0, 4), "M": (4, 4)}, {"M": (0, 4)})
LATE = (
    {"HB": (0, 4), "CB": (4, 3), "CT": (7, 1)},
    {"HT": (0, 2), "HB": (2, 4), "CB": (6, 3), "CT": (9, 1)},
)
SLOT = {"HB": 0, "HT": 1, "CB": 2, "CT": 3, "M": 4}
REACH = (3, 1)


def units(layout):
    return sum(count for _, count in layout.values())


def both(half):
    shift = units(SOON[half])
    near = dict(SOON[half])
    near.update({k: (o + shift, n) for k, (o, n) in LATE[half].items()})
    return near


def sigmoid(v):
    return 0.5 * jnp.tanh(0.5 * v) + 0.5


def taps_of(row):
    lane = lax.broadcasted_iota(jnp.int32, row.shape, 1)
    zero = jnp.zeros_like(row)
    before = jnp.where(lane == 0, zero, pltpu.roll(row, 1, 1))
    after = jnp.where(lane == GW - 1, zero, pltpu.roll(row, GW - 1, 1))
    return jnp.concatenate([before, row, after], axis=0)


def phase_kernel(plan, *refs):
    names = plan["names"]
    outs = plan["outs"]
    n_in = len(names)
    ref = dict(zip(names, refs[:n_in]))
    out = dict(zip(outs, refs[n_in : n_in + len(outs)]))
    tx, th, tm, tx2, th2, tm2, yb, ob, yb2, ob2, raw = refs[n_in + len(outs) :]
    state_out = out["state"]
    core = ref["sc"][0]
    top = ref["sc"][1]
    first_core = core == 0

    def keep(row, value):
        if 0 <= row < OWN:
            return value
        g = top + row
        return jnp.where(jnp.logical_and(g >= 0, g < 128), value, jnp.zeros_like(value))

    def fetch(field, row):
        (own, slot), (near, near_at, far, far_at, count) = plan["fields"][field]
        if 0 <= row < OWN:
            return ref[own][slot, row]
        if row < 0:
            unit = count + row
            value = jnp.where(first_core, ref[far][far_at + unit], ref[near][near_at + unit])
        else:
            unit = row - OWN
            value = jnp.where(first_core, ref[near][near_at + unit], ref[far][far_at + unit])
        return keep(row, value)

    rows_of = [list(range(-reach, OWN + reach)) for reach in REACH]
    bufs = ((tx, th, tm, yb, ob), (tx2, th2, tm2.at[1:9], yb2, ob2))
    filled = set()

    def fill(buf, key, field, reach, upto):
        for i in range(upto):
            if (key, i) not in filled:
                filled.add((key, i))
                buf[i] = taps_of(fetch(field, i - reach))

    def matmuls(index, q):
        bx, bh, bm, _, _ = bufs[index]
        if index == 0:
            fill(tx, "x", "X", 4, q + 4)
            fill(th, "h", "HB", 4, q + 4)
            fill(tm, "m", "M", 4, q + 4)
        else:
            fill(th2, "h2", "HT", 2, q + 4)
        cols = [
            jnp.concatenate([buf[i + a] for buf in (bx, bh, bm) for a in range(3)], axis=0)
            for i in (q, q + 1)
        ]
        rhs = jnp.concatenate(cols, axis=1)
        x, h, m = rhs[0:576], rhs[576:1152], rhs[1152:1728]
        layer = plan["layer"] + index
        shared = jnp.dot(
            ref["wb"][layer],
            jnp.concatenate([x, h[512:576], m[0:128]], axis=0),
            preferred_element_type=F32,
        )
        slot = (q // 2 + index) % 2
        raw[slot, 0:256] = shared[0:256] + jnp.dot(
            ref["wa"][layer], h[0:512], preferred_element_type=F32
        )
        raw[slot, 256:448] = shared[256:448] + jnp.dot(
            ref["wc"][layer], m[128:576], preferred_element_type=F32
        )
        return raw.at[slot, 0:256], raw.at[slot, 256:448]

    def gates(index, q, acc1, acc2):
        _, _, _, y_buf, o_buf = bufs[index]
        rows = rows_of[index]
        pair = (rows[q], rows[q + 1])
        c_field = "CT" if index else "CB"
        c_prev = jnp.concatenate([fetch(c_field, row) for row in pair], axis=1).astype(F32)
        if index:
            m_rows = [tm2[row + 3, 64:128] for row in pair]
        else:
            m_rows = [tm[row + 4, 64:128] for row in pair]
        m_prev = jnp.concatenate(m_rows, axis=1).astype(F32)
        c_new = sigmoid(acc1[64:128] + 1.0) * c_prev + sigmoid(acc1[0:64]) * jnp.tanh(acc1[128:192])
        m_new = sigmoid(acc2[64:128] + 1.0) * m_prev + sigmoid(acc2[0:64]) * jnp.tanh(acc2[128:192])
        c_new = c_new.astype(BF)
        m_new = m_new.astype(BF)
        lanes = slice(q * GW, (q + 2) * GW)
        o_buf[:, lanes] = acc1[192:256]
        blocks = []
        for j, row in enumerate(pair):
            c_row = keep(row, c_new[:, j * GW : (j + 1) * GW])
            m_row = keep(row, m_new[:, j * GW : (j + 1) * GW])
            if 0 <= row < OWN:
                state_out[SLOT[c_field], row] = c_row
                if index:
                    state_out[SLOT["M"], row] = m_row
            c_taps = taps_of(c_row)
            m_taps = taps_of(m_row)
            if not index:
                tm2[row + 3] = m_taps
            blocks.append(
                jnp.concatenate(
                    [t[64 * b : 64 * b + 64] for b in range(3) for t in (c_taps, m_taps)], axis=0
                )
            )
        y_buf[:, lanes] = jnp.dot(
            ref["wo"][plan["layer"] + index],
            jnp.concatenate(blocks, axis=1),
            preferred_element_type=F32,
        )

    def hidden(index, q):
        _, _, _, y_buf, o_buf = bufs[index]
        lanes = slice(q * GW, (q + 1) * GW)
        gate = (
            o_buf[:, lanes]
            + y_buf[0:64, (q - 1) * GW : q * GW]
            + y_buf[64:128, lanes]
            + y_buf[128:192, (q + 1) * GW : (q + 2) * GW]
        )
        h_new = (sigmoid(gate) * jnp.tanh(y_buf[192:256, lanes])).astype(BF)
        row = rows_of[index][q]
        h_new = keep(row, h_new)
        if 0 <= row < OWN:
            state_out[SLOT["HT" if index else "HB"], row] = h_new
        if not index:
            tx2[row + 2] = taps_of(h_new)

    def finish(index, q, accs):
        gates(index, q, *accs)
        for h in (q - 1, q):
            if h >= 1:
                hidden(index, h)

    tasks = [(i, q) for i in range(2) for q in range(0, len(rows_of[i]), 2)]
    waiting = None
    for task in tasks:
        accs = matmuls(*task)
        if waiting is not None:
            finish(*waiting)
        waiting = task + (accs,)
    finish(*waiting)

    def send(target, layout, last_rows_if):
        for field, (offset, count) in layout.items():
            for u in range(count):
                low = state_out[SLOT[field], u]
                high = state_out[SLOT[field], OWN - count + u]
                target[offset + u] = jnp.where(last_rows_if, high, low)

    half = plan["half"]
    if "give" in out:
        lower, slots = ref[plan["lower"]], out["give"].shape[0]
        for slot in range(slots):
            for row in range(OWN):
                out["give"][slot, row] = jnp.where(
                    first_core, state_out[slot, row], lower[slot, row]
                )
    if "near" in out:
        send(out["near"], both(half) if "late" in out else SOON[half], first_core)
    if "soon" in out:
        send(out["soon"], SOON[half], jnp.logical_not(first_core))
    if "late" in out:
        send(out["late"], LATE[half], jnp.logical_not(first_core))


def run_phase(operands, plan):
    names = list(operands)
    plan = dict(plan, names=names)
    unit = (CH, GW)
    half = plan["half"]
    sizes = {"state": (5, OWN) + unit}
    if plan["send"]:
        far = {"soon": units(SOON[half])}
        if plan["send"] > 1:
            far["late"] = units(LATE[half])
        sizes["near"] = (sum(far.values()),) + unit
        sizes.update({k: (n,) + unit for k, n in far.items()})
    else:
        sizes["give"] = sizes["state"]
    plan["outs"] = list(sizes)
    in_specs = [
        pl.BlockSpec(memory_space=pltpu.SMEM if name == "sc" else pltpu.VMEM) for name in names
    ]
    results = pl.pallas_call(
        functools.partial(phase_kernel, plan),
        out_shape=[jax.ShapeDtypeStruct(s, BF) for s in sizes.values()],
        in_specs=in_specs,
        out_specs=[pl.BlockSpec(memory_space=pltpu.VMEM) for _ in sizes],
        scratch_shapes=[
            pltpu.VMEM((12, 3 * CH, GW), BF),
            pltpu.VMEM((12, 3 * CH, GW), BF),
            pltpu.VMEM((12, 3 * CH, GW), BF),
            pltpu.VMEM((8, 3 * CH, GW), BF),
            pltpu.VMEM((8, 3 * CH, GW), BF),
            pltpu.VMEM((10, 3 * CH, GW), BF),
            pltpu.VMEM((4 * CH, 10 * GW), F32),
            pltpu.VMEM((CH, 10 * GW), F32),
            pltpu.VMEM((4 * CH, 6 * GW), F32),
            pltpu.VMEM((CH, 6 * GW), F32),
            pltpu.VMEM((2, 7 * CH, 2 * GW), F32),
        ],
        compiler_params=pltpu.CompilerParams(vmem_limit_bytes=24 << 20),
        name="two_layers",
    )(*[operands[name] for name in names])
    return dict(zip(sizes, results))


def pack_weights_kernel(sc, *refs):
    sources, (wa, wb, wc, wo) = refs[:10], refs[10:14]
    inputs, sems = refs[14:24], refs[24]
    core = sc[0]
    copies = [pltpu.make_async_copy(s, t, sems.at[i]) for i, (s, t) in enumerate(zip(sources, inputs))]
    for c in copies:
        c.start()
    for group in range(2):
        for c in copies[5 * group : 5 * group + 5]:
            c.wait()
        x, h, m, o, last = inputs[5 * group : 5 * group + 5]
        first = 2 * core if group == 0 else 2 - 2 * core
        for l in range(2):
            at = first + l
            xt = x[l]
            ht = jnp.transpose(h[l])
            mt = m[l]
            ot = o[l]
            wa[at] = ht[:, 0:512]
            wc[at] = mt[:, 128:576]
            gate_rows = jnp.concatenate([xt[0:192], xt[384:448]], axis=0)
            wb[at, 0:256, 0:512] = gate_rows[:, 0:512]
            wb[at, 0:256, 512:640] = jnp.concatenate([gate_rows[:, 512:576], ht[:, 512:576]], axis=1)
            wb[at, 0:256, 640:768] = jnp.zeros((256, 128), BF)
            wb[at, 256:448, 0:512] = xt[192:384, 0:512]
            wb[at, 256:448, 512:640] = jnp.concatenate(
                [xt[192:384, 512:576], jnp.zeros((192, 64), BF)], axis=1
            )
            wb[at, 256:448, 640:768] = mt[:, 0:128]
            for a in range(3):
                wo[at, 64 * a : 64 * a + 64] = ot[:, 384 * a : 384 * a + 384]
            wo[at, 192:256, 0:128] = jnp.zeros((64, 128), BF)
            wo[at, 192:256, 128:256] = last[l]
            wo[at, 192:256, 256:384] = jnp.zeros((64, 128), BF)


def pack_weights(scalars, own, other):
    shapes = ((4, 256, 512), (4, 448, 768), (4, 192, 448), (4, 256, 384))
    vmem = pl.BlockSpec(memory_space=pltpu.VMEM)
    return pl.pallas_call(
        pack_weights_kernel,
        out_shape=[jax.ShapeDtypeStruct(s, BF) for s in shapes],
        in_specs=[pl.BlockSpec(memory_space=pltpu.SMEM)]
        + [pl.BlockSpec(memory_space=pltpu.HBM)] * 10,
        out_specs=[vmem] * 4,
        scratch_shapes=[pltpu.VMEM(w.shape, BF) for w in (*own, *other)]
        + [pltpu.SemaphoreType.DMA((10,))],
        compiler_params=pltpu.CompilerParams(vmem_limit_bytes=32 << 20),
        name="pack_weights",
    )(scalars, *own, *other)


def cut_state_kernel(sc, *refs):
    sources, pieces, copied, sems = refs[:4], refs[4:8], refs[8:12], refs[12]
    copies = [pltpu.make_async_copy(s, t, sems.at[i]) for i, (s, t) in enumerate(zip(sources, copied))]
    for c in copies:
        c.start()
    for c in copies:
        c.wait()
    frames, hidden, cell, memory = copied
    first_core, z = sc[0] == 0, sc[2]
    for k in range(4):
        seq = lax.rem(z + k, 4)
        for i in range(2):
            for l in range(2):
                pieces[k][l, i] = hidden[l, seq, i]
                pieces[k][2 + l, i] = cell[l, seq, i]
            pieces[k][4, i] = jnp.where(first_core, memory[seq, i], frames[1, seq, i])
            pieces[k][5, i] = jnp.where(first_core, frames[0, seq, i], frames[2, seq, i])


def cut_state(scalars, frames, hidden, cell, memory):
    vmem = pl.BlockSpec(memory_space=pltpu.VMEM)
    return pl.pallas_call(
        cut_state_kernel,
        out_shape=[jax.ShapeDtypeStruct((6, 2, CH, GW), BF)] * 4,
        in_specs=[pl.BlockSpec(memory_space=pltpu.SMEM)]
        + [pl.BlockSpec(memory_space=pltpu.HBM)] * 4,
        out_specs=[vmem] * 4,
        scratch_shapes=[pltpu.VMEM(v.shape, BF) for v in (frames, hidden, cell, memory)]
        + [pltpu.SemaphoreType.DMA((4,))],
        compiler_params=pltpu.CompilerParams(vmem_limit_bytes=8 << 20),
        name="cut_state",
    )(scalars, frames, hidden, cell, memory)


ORDER_A = ((1, "HT"), (4, "M"), (0, "HB"), (2, "CB"), (3, "CT"), (5, "F0"))
ORDER_B = ((1, "HT"), (0, "HB"), (2, "CB"), (3, "CT"), (4, "F1"), (5, "F2"))


def open_state_kernel(sc, *refs):
    mine, theirs = refs[:4], refs[4:8]
    low_own, high_own, near_a, near_b, far_a, far_b, rows = refs[8:]
    core, z = sc[0], sc[2]
    for k in range(4):
        at = 2 * lax.rem(z + 4 - k, 4)
        for i in range(2):
            for a in range(6):
                rows[0, a, at + i] = mine[k][a, i]
                rows[1, a, at + i] = theirs[k][a, i]
    other = 1 - core
    for a in range(6):
        for r in range(OWN):
            low_own[a, r] = rows[core, a, 4 * core + r]
            high_own[a, r] = rows[other, a, 4 * core + r]
    for group, order, layout, near, far in (
        (core, ORDER_A, FIRST_A, near_a, far_a),
        (other, ORDER_B, FIRST_B, near_b, far_b),
    ):
        for a, name in order:
            offset, count = layout[name]
            for u in range(count):
                turn = core * (OWN - count) + u
                far[offset + u] = rows[group, a, 4 * core + turn]
                near[offset + u] = rows[group, a, 4 * other + turn]


def open_state(scalars, mine, theirs):
    vmem = pl.BlockSpec(memory_space=pltpu.VMEM)
    shapes = [(6, OWN)] * 2 + [(18,)] * 4
    return pl.pallas_call(
        open_state_kernel,
        out_shape=[jax.ShapeDtypeStruct(s + (CH, GW), BF) for s in shapes],
        in_specs=[pl.BlockSpec(memory_space=pltpu.SMEM)] + [vmem] * 8,
        out_specs=[vmem] * 6,
        scratch_shapes=[pltpu.VMEM((2, 6, 8, CH, GW), BF)],
        compiler_params=pltpu.CompilerParams(vmem_limit_bytes=16 << 20),
        name="open_state",
    )(scalars, *mine, *theirs)


def cut_result_kernel(sc, low, high, taken, *pieces):
    core, z = sc[0], sc[2]
    for k in range(4):
        to = lax.rem(z + k, 4)
        here = (to // 2) == core
        row = 2 * lax.rem(to, 2)
        for a in range(5):
            for i in range(2):
                own = jnp.where(core == 0, low[a, row + i], high[a, row + i])
                pieces[k][a, i] = jnp.where(here, own, taken[a, row + i])


def cut_result(scalars, low, high, taken):
    vmem = pl.BlockSpec(memory_space=pltpu.VMEM)
    return pl.pallas_call(
        cut_result_kernel,
        out_shape=[jax.ShapeDtypeStruct((5, 2, CH, GW), BF)] * 4,
        in_specs=[pl.BlockSpec(memory_space=pltpu.SMEM)] + [vmem] * 3,
        out_specs=[vmem] * 4,
        compiler_params=pltpu.CompilerParams(vmem_limit_bytes=8 << 20),
        name="cut_result",
    )(scalars, low, high, taken)


def close_result_kernel(sc, *refs):
    parts = refs[:4]
    hidden, cell, memory = refs[4:]
    z = sc[2]
    for k in range(4):
        seq = lax.rem(z + 4 - k, 4)
        for i in range(2):
            for a in range(2):
                hidden[a, seq, i] = parts[k][a, i]
                cell[a, seq, i] = parts[k][2 + a, i]
            memory[0, seq, i] = parts[k][4, i]


def close_result(scalars, parts):
    vmem = pl.BlockSpec(memory_space=pltpu.VMEM)
    shapes = ((2, 4, 2), (2, 4, 2), (1, 4, 2))
    return pl.pallas_call(
        close_result_kernel,
        out_shape=[jax.ShapeDtypeStruct(s + (CH, GW), BF) for s in shapes],
        in_specs=[pl.BlockSpec(memory_space=pltpu.SMEM)] + [vmem] * 4,
        out_specs=[vmem] * 3,
        compiler_params=pltpu.CompilerParams(vmem_limit_bytes=8 << 20),
        name="close_result",
    )(scalars, *parts)


def program(frames, hidden_in, cell_in, memory_in, w_x, w_h, w_m, w_o, w_last):
    core = lax.axis_index("layer")
    chip = lax.axis_index("rows")
    chips = lax.axis_size("rows")
    swap = [(0, 1), (1, 0)]
    across = []
    for i in range(chips):
        across.append((chips + i, (i + 4) % chips))
        across.append((i, chips + (i - 4) % chips))

    def to_partner(value):
        return lax.ppermute(value, "layer", swap)

    def to_neighbour(value):
        return lax.ppermute(value, ("layer", "rows"), across)

    def around(value, k):
        turn = [(i, 4 * (i // 4) + (i + k) % 4) for i in range(chips)]
        return lax.ppermute(value, "rows", turn)

    scalars = jnp.stack([core, 8 * (chip // 4) + 4 * core, chip % 4]).astype(jnp.int32)
    turned = [jnp.swapaxes(w, 1, 2) for w in (w_x, w_m, w_o, w_last)]
    scalars, own_w = lax.optimization_barrier(
        (scalars, [turned[0], w_h, turned[1], turned[2], turned[3]])
    )
    other_w = [to_partner(w) for w in own_w]
    wa, wb, wc, wo = pack_weights(scalars, own_w, other_w)

    pieces = cut_state(scalars, frames, hidden_in, cell_in, memory_in)
    mine = [pieces[0]] + [around(pieces[k], k) for k in (1, 2, 3)]
    theirs = [to_partner(piece) for piece in mine]
    low_own, high_own, near_a, near_b, message_a, message_b = open_state(scalars, mine, theirs)
    far_a = to_neighbour(message_a)
    far_b = to_neighbour(message_b)

    base = {"sc": scalars, "wa": wa, "wb": wb, "wc": wc, "wo": wo}
    arrays = {"s00": low_own, "s01": high_own, "na": near_a, "fa": far_a, "nb": near_b, "fb": far_b}

    def first(letter, layout, field):
        offset, count = layout[field]
        return ("n" + letter, offset, "f" + letter, offset, count)

    kept = ("HB", "HT", "CB", "CT")
    halo = [{k: first("a", FIRST_A, k) for k in kept}, {k: first("b", FIRST_B, k) for k in kept}]
    states = ["s00", "s01"]
    own_m = ("s00", 4)
    halo_m = first("a", FIRST_A, "M")
    frame_field = (
        (("s00", 5), first("a", FIRST_A, "F0")),
        (("s01", 4), first("b", FIRST_B, "F1")),
        (("s01", 5), first("b", FIRST_B, "F2")),
    )
    steps = frames.shape[0]
    results = [None, None]
    for step in range(steps):
        x_field = frame_field[step]
        for half in range(2):
            send = 2 if step < steps - 1 else 1 - half
            fields = {k: ((states[half], SLOT[k]), halo[half][k]) for k in kept}
            fields["M"] = (own_m, halo_m)
            fields["X"] = x_field
            needed = {f[0][0] for f in fields.values()}
            needed |= {f[1][i] for f in fields.values() for i in (0, 2)}
            operands = dict(base)
            for name in sorted(needed):
                operands[name] = arrays[name]
            plan = {"fields": fields, "half": half, "layer": 2 * half, "send": send}
            if not send:
                plan["lower"] = states[0]
                operands[states[0]] = arrays[states[0]]
            tag = f"{step}{half}"
            outs = run_phase(operands, plan)
            results[half] = outs["state"]
            states[half] = "state" + tag
            arrays["state" + tag] = outs["state"]
            own_m = ("state" + tag, SLOT["M"])
            if send:
                arrays["soon" + tag] = to_neighbour(outs["soon"])
                arrays["near" + tag] = to_partner(outs["near"])
                near_at = both(half)
                for k, (o, n) in SOON[half].items():
                    spec = ("near" + tag, near_at[k][0], "soon" + tag, o, n)
                    if k == "M":
                        halo_m = spec
                    else:
                        x_field = (("state" + tag, SLOT["HT"]), spec)
                        halo[half][k] = spec
            if send > 1:
                arrays["late" + tag] = to_neighbour(outs["late"])
                for k, (o, n) in LATE[half].items():
                    halo[half][k] = ("near" + tag, near_at[k][0], "late" + tag, o, n)

    taken = to_partner(outs["give"])
    pieces = cut_result(scalars, results[0], results[1], taken)
    done = [pieces[0]] + [around(pieces[k], k) for k in (1, 2, 3)]
    return tuple(close_result(scalars, done))


def solution(mesh):
    return jax.shard_map(
        program,
        mesh=mesh,
        in_specs=(
            P(None, None, "rows", None, None),
            P("layer", None, "rows", None, None),
            P("layer", None, "rows", None, None),
            P(None, "rows", None, None),
            P("layer", None, None),
            P("layer", None, None),
            P("layer", None, None),
            P("layer", None, None),
            P("layer", None, None),
        ),
        out_specs=(
            P("layer", None, "rows", None, None),
            P("layer", None, "rows", None, None),
            P("layer", None, "rows", None, None),
        ),
        check_vma=False,
    )
```

```python
import functools

import jax
import jax.numpy as jnp
from jax import lax
from jax.experimental import pallas as pl
from jax.experimental.pallas import tpu as pltpu
from jax.sharding import PartitionSpec as P


CH = 64
GW = 128
OWN = 4
BF = jnp.bfloat16
F32 = jnp.float32

FIRST_A = {"HT": (0, 2), "M": (2, 4), "HB": (6, 4), "CB": (10, 3), "CT": (13, 1), "F0": (14, 4)}
FIRST_B = {"HT": (0, 2), "HB": (2, 4), "CB": (6, 3), "CT": (9, 1), "F1": (10, 4), "F2": (14, 4)}
SOON = ({"HT": (0, 4), "M": (4, 4)}, {"M": (0, 4)})
LATE = (
    {"HB": (0, 4), "CB": (4, 3), "CT": (7, 1)},
    {"HT": (0, 2), "HB": (2, 4), "CB": (6, 3), "CT": (9, 1)},
)
SLOT = {"HB": 0, "HT": 1, "CB": 2, "CT": 3, "M": 4}
REACH = (3, 1)


def units(layout):
    return sum(count for _, count in layout.values())


def both(half):
    shift = units(SOON[half])
    near = dict(SOON[half])
    near.update({k: (o + shift, n) for k, (o, n) in LATE[half].items()})
    return near


def sigmoid(v):
    return 0.5 * jnp.tanh(0.5 * v) + 0.5


def taps_of(row):
    lane = lax.broadcasted_iota(jnp.int32, row.shape, 1)
    zero = jnp.zeros_like(row)
    before = jnp.where(lane == 0, zero, pltpu.roll(row, 1, 1))
    after = jnp.where(lane == GW - 1, zero, pltpu.roll(row, GW - 1, 1))
    return jnp.concatenate([before, row, after], axis=0)


def phase_kernel(plan, *refs):
    names = plan["names"]
    outs = plan["outs"]
    n_in = len(names)
    ref = dict(zip(names, refs[:n_in]))
    out = dict(zip(outs, refs[n_in : n_in + len(outs)]))
    tx, th, tm, tx2, th2, tm2, yb, ob, yb2, ob2, raw = refs[n_in + len(outs) :]
    state_out = out["state"]
    core = ref["sc"][0]
    top = ref["sc"][1]
    first_core = core == 0

    def keep(row, value):
        if 0 <= row < OWN:
            return value
        g = top + row
        return jnp.where(jnp.logical_and(g >= 0, g < 128), value, jnp.zeros_like(value))

    def fetch(field, row):
        (own, slot), (near, near_at, far, far_at, count) = plan["fields"][field]
        if 0 <= row < OWN:
            return ref[own][slot, row]
        if row < 0:
            unit = count + row
            value = jnp.where(first_core, ref[far][far_at + unit], ref[near][near_at + unit])
        else:
            unit = row - OWN
            value = jnp.where(first_core, ref[near][near_at + unit], ref[far][far_at + unit])
        return keep(row, value)

    rows_of = [list(range(-reach, OWN + reach)) for reach in REACH]
    bufs = ((tx, th, tm, yb, ob), (tx2, th2, tm2.at[1:9], yb2, ob2))
    filled = set()

    def fill(buf, key, field, reach, upto):
        for i in range(upto):
            if (key, i) not in filled:
                filled.add((key, i))
                buf[i] = taps_of(fetch(field, i - reach))

    def matmuls(index, q):
        bx, bh, bm, _, _ = bufs[index]
        if index == 0:
            fill(tx, "x", "X", 4, q + 4)
            fill(th, "h", "HB", 4, q + 4)
            fill(tm, "m", "M", 4, q + 4)
        else:
            fill(th2, "h2", "HT", 2, q + 4)
        cols = [
            jnp.concatenate([buf[i + a] for buf in (bx, bh, bm) for a in range(3)], axis=0)
            for i in (q, q + 1)
        ]
        rhs = jnp.concatenate(cols, axis=1)
        x, h, m = rhs[0:576], rhs[576:1152], rhs[1152:1728]
        layer = plan["layer"] + index
        shared = jnp.dot(
            ref["wb"][layer],
            jnp.concatenate([x, h[512:576], m[0:128]], axis=0),
            preferred_element_type=F32,
        )
        slot = (q // 2 + index) % 2
        raw[slot, 0:256] = shared[0:256] + jnp.dot(
            ref["wa"][layer], h[0:512], preferred_element_type=F32
        )
        raw[slot, 256:448] = shared[256:448] + jnp.dot(
            ref["wc"][layer], m[128:576], preferred_element_type=F32
        )
        return raw.at[slot, 0:256], raw.at[slot, 256:448]

    def gates(index, q, acc1, acc2):
        _, _, _, y_buf, o_buf = bufs[index]
        rows = rows_of[index]
        pair = (rows[q], rows[q + 1])
        c_field = "CT" if index else "CB"
        c_prev = jnp.concatenate([fetch(c_field, row) for row in pair], axis=1).astype(F32)
        if index:
            m_rows = [tm2[row + 3, 64:128] for row in pair]
        else:
            m_rows = [tm[row + 4, 64:128] for row in pair]
        m_prev = jnp.concatenate(m_rows, axis=1).astype(F32)
        c_new = sigmoid(acc1[64:128] + 1.0) * c_prev + sigmoid(acc1[0:64]) * jnp.tanh(acc1[128:192])
        m_new = sigmoid(acc2[64:128] + 1.0) * m_prev + sigmoid(acc2[0:64]) * jnp.tanh(acc2[128:192])
        c_new = c_new.astype(BF)
        m_new = m_new.astype(BF)
        lanes = slice(q * GW, (q + 2) * GW)
        o_buf[:, lanes] = acc1[192:256]
        blocks = []
        for j, row in enumerate(pair):
            c_row = keep(row, c_new[:, j * GW : (j + 1) * GW])
            m_row = keep(row, m_new[:, j * GW : (j + 1) * GW])
            if 0 <= row < OWN:
                state_out[SLOT[c_field], row] = c_row
                if index:
                    state_out[SLOT["M"], row] = m_row
            c_taps = taps_of(c_row)
            m_taps = taps_of(m_row)
            if not index:
                tm2[row + 3] = m_taps
            blocks.append(
                jnp.concatenate(
                    [t[64 * b : 64 * b + 64] for b in range(3) for t in (c_taps, m_taps)], axis=0
                )
            )
        y_buf[:, lanes] = jnp.dot(
            ref["wo"][plan["layer"] + index],
            jnp.concatenate(blocks, axis=1),
            preferred_element_type=F32,
        )

    def hidden(index, q):
        _, _, _, y_buf, o_buf = bufs[index]
        lanes = slice(q * GW, (q + 1) * GW)
        gate = (
            o_buf[:, lanes]
            + y_buf[0:64, (q - 1) * GW : q * GW]
            + y_buf[64:128, lanes]
            + y_buf[128:192, (q + 1) * GW : (q + 2) * GW]
        )
        h_new = (sigmoid(gate) * jnp.tanh(y_buf[192:256, lanes])).astype(BF)
        row = rows_of[index][q]
        h_new = keep(row, h_new)
        if 0 <= row < OWN:
            state_out[SLOT["HT" if index else "HB"], row] = h_new
        if not index:
            tx2[row + 2] = taps_of(h_new)

    def finish(index, q, accs):
        gates(index, q, *accs)
        for h in (q - 1, q):
            if h >= 1:
                hidden(index, h)

    tasks = [(i, q) for i in range(2) for q in range(0, len(rows_of[i]), 2)]
    waiting = None
    for task in tasks:
        accs = matmuls(*task)
        if waiting is not None:
            finish(*waiting)
        waiting = task + (accs,)
    finish(*waiting)

    def send(target, layout, last_rows_if):
        for field, (offset, count) in layout.items():
            for u in range(count):
                low = state_out[SLOT[field], u]
                high = state_out[SLOT[field], OWN - count + u]
                target[offset + u] = jnp.where(last_rows_if, high, low)

    half = plan["half"]
    if "give" in out:
        lower, slots = ref[plan["lower"]], out["give"].shape[0]
        for slot in range(slots):
            for row in range(OWN):
                out["give"][slot, row] = jnp.where(
                    first_core, state_out[slot, row], lower[slot, row]
                )
    if "near" in out:
        send(out["near"], both(half) if "late" in out else SOON[half], first_core)
    if "soon" in out:
        send(out["soon"], SOON[half], jnp.logical_not(first_core))
    if "late" in out:
        send(out["late"], LATE[half], jnp.logical_not(first_core))


def run_phase(operands, plan):
    names = list(operands)
    plan = dict(plan, names=names)
    unit = (CH, GW)
    half = plan["half"]
    sizes = {"state": (5, OWN) + unit}
    if plan["send"]:
        far = {"soon": units(SOON[half])}
        if plan["send"] > 1:
            far["late"] = units(LATE[half])
        sizes["near"] = (sum(far.values()),) + unit
        sizes.update({k: (n,) + unit for k, n in far.items()})
    else:
        sizes["give"] = sizes["state"]
    plan["outs"] = list(sizes)
    in_specs = [
        pl.BlockSpec(memory_space=pltpu.SMEM if name == "sc" else pltpu.VMEM) for name in names
    ]
    results = pl.pallas_call(
        functools.partial(phase_kernel, plan),
        out_shape=[jax.ShapeDtypeStruct(s, BF) for s in sizes.values()],
        in_specs=in_specs,
        out_specs=[pl.BlockSpec(memory_space=pltpu.VMEM) for _ in sizes],
        scratch_shapes=[
            pltpu.VMEM((12, 3 * CH, GW), BF),
            pltpu.VMEM((12, 3 * CH, GW), BF),
            pltpu.VMEM((12, 3 * CH, GW), BF),
            pltpu.VMEM((8, 3 * CH, GW), BF),
            pltpu.VMEM((8, 3 * CH, GW), BF),
            pltpu.VMEM((10, 3 * CH, GW), BF),
            pltpu.VMEM((4 * CH, 10 * GW), F32),
            pltpu.VMEM((CH, 10 * GW), F32),
            pltpu.VMEM((4 * CH, 6 * GW), F32),
            pltpu.VMEM((CH, 6 * GW), F32),
            pltpu.VMEM((2, 7 * CH, 2 * GW), F32),
        ],
        compiler_params=pltpu.CompilerParams(vmem_limit_bytes=24 << 20),
        name="two_layers",
    )(*[operands[name] for name in names])
    return dict(zip(sizes, results))


def in_hbm(*values):
    return [pltpu.with_memory_space_constraint(v, pltpu.HBM) for v in values]


def pack_weights_kernel(sc, *refs):
    sources, (wa, wb, wc, wo) = refs[:10], refs[10:14]
    inputs, sems = refs[14:24], refs[24]
    core = sc[0]
    copies = [pltpu.make_async_copy(s, t, sems.at[i]) for i, (s, t) in enumerate(zip(sources, inputs))]
    for c in copies:
        c.start()
    for group in range(2):
        for c in copies[5 * group : 5 * group + 5]:
            c.wait()
        x, h, m, o, last = inputs[5 * group : 5 * group + 5]
        first = 2 * core if group == 0 else 2 - 2 * core
        for l in range(2):
            at = first + l
            xt = x[l]
            ht = jnp.transpose(h[l])
            mt = m[l]
            ot = o[l]
            wa[at] = ht[:, 0:512]
            wc[at] = mt[:, 128:576]
            gate_rows = jnp.concatenate([xt[0:192], xt[384:448]], axis=0)
            wb[at, 0:256, 0:512] = gate_rows[:, 0:512]
            wb[at, 0:256, 512:640] = jnp.concatenate([gate_rows[:, 512:576], ht[:, 512:576]], axis=1)
            wb[at, 0:256, 640:768] = jnp.zeros((256, 128), BF)
            wb[at, 256:448, 0:512] = xt[192:384, 0:512]
            wb[at, 256:448, 512:640] = jnp.concatenate(
                [xt[192:384, 512:576], jnp.zeros((192, 64), BF)], axis=1
            )
            wb[at, 256:448, 640:768] = mt[:, 0:128]
            for a in range(3):
                wo[at, 64 * a : 64 * a + 64] = ot[:, 384 * a : 384 * a + 384]
            wo[at, 192:256, 0:128] = jnp.zeros((64, 128), BF)
            wo[at, 192:256, 128:256] = last[l]
            wo[at, 192:256, 256:384] = jnp.zeros((64, 128), BF)


def pack_weights(scalars, own, other):
    shapes = ((4, 256, 512), (4, 448, 768), (4, 192, 448), (4, 256, 384))
    vmem = pl.BlockSpec(memory_space=pltpu.VMEM)
    return pl.pallas_call(
        pack_weights_kernel,
        out_shape=[jax.ShapeDtypeStruct(s, BF) for s in shapes],
        in_specs=[pl.BlockSpec(memory_space=pltpu.SMEM)]
        + [pl.BlockSpec(memory_space=pltpu.HBM)] * 10,
        out_specs=[vmem] * 4,
        scratch_shapes=[pltpu.VMEM(w.shape, BF) for w in (*own, *other)]
        + [pltpu.SemaphoreType.DMA((10,))],
        compiler_params=pltpu.CompilerParams(vmem_limit_bytes=32 << 20),
        name="pack_weights",
    )(scalars, *in_hbm(*own), *other)


def cut_state_kernel(sc, *refs):
    sources, pieces, copied, sems = refs[:4], refs[4:8], refs[8:12], refs[12]
    copies = [pltpu.make_async_copy(s, t, sems.at[i]) for i, (s, t) in enumerate(zip(sources, copied))]
    for c in copies:
        c.start()
    for c in copies:
        c.wait()
    frames, hidden, cell, memory = copied
    first_core, z = sc[0] == 0, sc[2]
    for k in range(4):
        seq = lax.rem(z + k, 4)
        for i in range(2):
            for l in range(2):
                pieces[k][l, i] = hidden[l, seq, i]
                pieces[k][2 + l, i] = cell[l, seq, i]
            pieces[k][4, i] = jnp.where(first_core, memory[seq, i], frames[1, seq, i])
            pieces[k][5, i] = jnp.where(first_core, frames[0, seq, i], frames[2, seq, i])


def cut_state(scalars, frames, hidden, cell, memory):
    vmem = pl.BlockSpec(memory_space=pltpu.VMEM)
    return pl.pallas_call(
        cut_state_kernel,
        out_shape=[jax.ShapeDtypeStruct((6, 2, CH, GW), BF)] * 4,
        in_specs=[pl.BlockSpec(memory_space=pltpu.SMEM)]
        + [pl.BlockSpec(memory_space=pltpu.HBM)] * 4,
        out_specs=[vmem] * 4,
        scratch_shapes=[pltpu.VMEM(v.shape, BF) for v in (frames, hidden, cell, memory)]
        + [pltpu.SemaphoreType.DMA((4,))],
        compiler_params=pltpu.CompilerParams(vmem_limit_bytes=8 << 20),
        name="cut_state",
    )(scalars, *in_hbm(frames, hidden, cell, memory))


ORDER_A = ((1, "HT"), (4, "M"), (0, "HB"), (2, "CB"), (3, "CT"), (5, "F0"))
ORDER_B = ((1, "HT"), (0, "HB"), (2, "CB"), (3, "CT"), (4, "F1"), (5, "F2"))


def open_state_kernel(sc, *refs):
    mine, theirs = refs[:4], refs[4:8]
    low_own, high_own, near_a, near_b, far_a, far_b, rows = refs[8:]
    core, z = sc[0], sc[2]
    for k in range(4):
        at = 2 * lax.rem(z + 4 - k, 4)
        for i in range(2):
            for a in range(6):
                rows[0, a, at + i] = mine[k][a, i]
                rows[1, a, at + i] = theirs[k][a, i]
    other = 1 - core
    for a in range(6):
        for r in range(OWN):
            low_own[a, r] = rows[core, a, 4 * core + r]
            high_own[a, r] = rows[other, a, 4 * core + r]
    for group, order, layout, near, far in (
        (core, ORDER_A, FIRST_A, near_a, far_a),
        (other, ORDER_B, FIRST_B, near_b, far_b),
    ):
        for a, name in order:
            offset, count = layout[name]
            for u in range(count):
                turn = core * (OWN - count) + u
                far[offset + u] = rows[group, a, 4 * core + turn]
                near[offset + u] = rows[group, a, 4 * other + turn]


def open_state(scalars, mine, theirs):
    vmem = pl.BlockSpec(memory_space=pltpu.VMEM)
    shapes = [(6, OWN)] * 2 + [(18,)] * 4
    return pl.pallas_call(
        open_state_kernel,
        out_shape=[jax.ShapeDtypeStruct(s + (CH, GW), BF) for s in shapes],
        in_specs=[pl.BlockSpec(memory_space=pltpu.SMEM)] + [vmem] * 8,
        out_specs=[vmem] * 6,
        scratch_shapes=[pltpu.VMEM((2, 6, 8, CH, GW), BF)],
        compiler_params=pltpu.CompilerParams(vmem_limit_bytes=16 << 20),
        name="open_state",
    )(scalars, *mine, *theirs)


def cut_result_kernel(sc, low, high, taken, *pieces):
    core, z = sc[0], sc[2]
    for k in range(4):
        to = lax.rem(z + k, 4)
        here = (to // 2) == core
        row = 2 * lax.rem(to, 2)
        for a in range(5):
            for i in range(2):
                own = jnp.where(core == 0, low[a, row + i], high[a, row + i])
                pieces[k][a, i] = jnp.where(here, own, taken[a, row + i])


def cut_result(scalars, low, high, taken):
    vmem = pl.BlockSpec(memory_space=pltpu.VMEM)
    return pl.pallas_call(
        cut_result_kernel,
        out_shape=[jax.ShapeDtypeStruct((5, 2, CH, GW), BF)] * 4,
        in_specs=[pl.BlockSpec(memory_space=pltpu.SMEM)] + [vmem] * 3,
        out_specs=[vmem] * 4,
        compiler_params=pltpu.CompilerParams(vmem_limit_bytes=8 << 20),
        name="cut_result",
    )(scalars, low, high, taken)


def close_result_kernel(sc, *refs):
    parts = refs[:4]
    hidden, cell, memory = refs[4:]
    z = sc[2]
    for k in range(4):
        seq = lax.rem(z + 4 - k, 4)
        for i in range(2):
            for a in range(2):
                hidden[a, seq, i] = parts[k][a, i]
                cell[a, seq, i] = parts[k][2 + a, i]
            memory[0, seq, i] = parts[k][4, i]


def close_result(scalars, parts):
    vmem = pl.BlockSpec(memory_space=pltpu.VMEM)
    shapes = ((2, 4, 2), (2, 4, 2), (1, 4, 2))
    return pl.pallas_call(
        close_result_kernel,
        out_shape=[jax.ShapeDtypeStruct(s + (CH, GW), BF) for s in shapes],
        in_specs=[pl.BlockSpec(memory_space=pltpu.SMEM)] + [vmem] * 4,
        out_specs=[vmem] * 3,
        compiler_params=pltpu.CompilerParams(vmem_limit_bytes=8 << 20),
        name="close_result",
    )(scalars, *parts)


def program(frames, hidden_in, cell_in, memory_in, w_x, w_h, w_m, w_o, w_last):
    core = lax.axis_index("layer")
    chip = lax.axis_index("rows")
    chips = lax.axis_size("rows")
    swap = [(0, 1), (1, 0)]
    across = []
    for i in range(chips):
        across.append((chips + i, i + 4 if i + 4 < chips else chips + (i ^ 1)))
        across.append((i, chips + i - 4 if i >= 4 else i ^ 1))

    def to_partner(value):
        return lax.ppermute(value, "layer", swap)

    def to_neighbour(value):
        return lax.ppermute(value, ("layer", "rows"), across)

    def around(value, k):
        turn = [(i, 4 * (i // 4) + (i + k) % 4) for i in range(chips)]
        return lax.ppermute(value, "rows", turn)

    scalars = jnp.stack([core, 8 * (chip // 4) + 4 * core, chip % 4]).astype(jnp.int32)
    turned = [jnp.swapaxes(w, 1, 2) for w in (w_x, w_m, w_o, w_last)]
    scalars, own_w = lax.optimization_barrier(
        (scalars, [turned[0], w_h, turned[1], turned[2], turned[3]])
    )
    other_w = [to_partner(w) for w in own_w]
    wa, wb, wc, wo = pack_weights(scalars, own_w, other_w)

    pieces = cut_state(scalars, frames, hidden_in, cell_in, memory_in)
    mine = [pieces[0]] + [around(pieces[k], k) for k in (1, 2, 3)]
    theirs = [to_partner(piece) for piece in mine]
    low_own, high_own, near_a, near_b, message_a, message_b = open_state(scalars, mine, theirs)
    far_a = to_neighbour(message_a)
    far_b = to_neighbour(message_b)

    base = {"sc": scalars, "wa": wa, "wb": wb, "wc": wc, "wo": wo}
    arrays = {"s00": low_own, "s01": high_own, "na": near_a, "fa": far_a, "nb": near_b, "fb": far_b}

    def first(letter, layout, field):
        offset, count = layout[field]
        return ("n" + letter, offset, "f" + letter, offset, count)

    kept = ("HB", "HT", "CB", "CT")
    halo = [{k: first("a", FIRST_A, k) for k in kept}, {k: first("b", FIRST_B, k) for k in kept}]
    states = ["s00", "s01"]
    own_m = ("s00", 4)
    halo_m = first("a", FIRST_A, "M")
    frame_field = (
        (("s00", 5), first("a", FIRST_A, "F0")),
        (("s01", 4), first("b", FIRST_B, "F1")),
        (("s01", 5), first("b", FIRST_B, "F2")),
    )
    steps = frames.shape[0]
    results = [None, None]
    for step in range(steps):
        x_field = frame_field[step]
        for half in range(2):
            send = 2 if step < steps - 1 else 1 - half
            fields = {k: ((states[half], SLOT[k]), halo[half][k]) for k in kept}
            fields["M"] = (own_m, halo_m)
            fields["X"] = x_field
            needed = {f[0][0] for f in fields.values()}
            needed |= {f[1][i] for f in fields.values() for i in (0, 2)}
            operands = dict(base)
            for name in sorted(needed):
                operands[name] = arrays[name]
            plan = {"fields": fields, "half": half, "layer": 2 * half, "send": send}
            if not send:
                plan["lower"] = states[0]
                operands[states[0]] = arrays[states[0]]
            tag = f"{step}{half}"
            outs = run_phase(operands, plan)
            results[half] = outs["state"]
            states[half] = "state" + tag
            arrays["state" + tag] = outs["state"]
            own_m = ("state" + tag, SLOT["M"])
            if send:
                arrays["soon" + tag] = to_neighbour(outs["soon"])
                arrays["near" + tag] = to_partner(outs["near"])
                near_at = both(half)
                for k, (o, n) in SOON[half].items():
                    spec = ("near" + tag, near_at[k][0], "soon" + tag, o, n)
                    if k == "M":
                        halo_m = spec
                    else:
                        x_field = (("state" + tag, SLOT["HT"]), spec)
                        halo[half][k] = spec
            if send > 1:
                arrays["late" + tag] = to_neighbour(outs["late"])
                for k, (o, n) in LATE[half].items():
                    halo[half][k] = ("near" + tag, near_at[k][0], "late" + tag, o, n)

    taken = to_partner(outs["give"])
    pieces = cut_result(scalars, results[0], results[1], taken)
    done = [pieces[0]] + [around(pieces[k], k) for k in (1, 2, 3)]
    return tuple(close_result(scalars, done))


def solution(mesh):
    return jax.shard_map(
        program,
        mesh=mesh,
        in_specs=(
            P(None, None, "rows", None, None),
            P("layer", None, "rows", None, None),
            P("layer", None, "rows", None, None),
            P(None, "rows", None, None),
            P("layer", None, None),
            P("layer", None, None),
            P("layer", None, None),
            P("layer", None, None),
            P("layer", None, None),
        ),
        out_specs=(
            P("layer", None, "rows", None, None),
            P("layer", None, "rows", None, None),
            P("layer", None, "rows", None, None),
        ),
        check_vma=False,
    )
```

```python
import functools

import jax
import jax.numpy as jnp
from jax import lax
from jax.experimental import pallas as pl
from jax.experimental.pallas import tpu as pltpu
from jax.sharding import PartitionSpec as P


CH = 64
GW = 128
OWN = 4
BF = jnp.bfloat16
F32 = jnp.float32

FIRST_A = {"HT": (0, 2), "M": (2, 4), "HB": (6, 4), "CB": (10, 3), "CT": (13, 1), "F0": (14, 4)}
FIRST_B = {"HT": (0, 2), "HB": (2, 4), "CB": (6, 3), "CT": (9, 1), "F1": (10, 4), "F2": (14, 4)}
SOON = ({"HT": (0, 4), "M": (4, 4)}, {"M": (0, 4)})
LATE = (
    {"HB": (0, 4), "CB": (4, 3), "CT": (7, 1)},
    {"HT": (0, 2), "HB": (2, 4), "CB": (6, 3), "CT": (9, 1)},
)
SLOT = {"HB": 0, "HT": 1, "CB": 2, "CT": 3, "M": 4}
REACH = (3, 1)


def units(layout):
    return sum(count for _, count in layout.values())


def both(half):
    shift = units(SOON[half])
    near = dict(SOON[half])
    near.update({k: (o + shift, n) for k, (o, n) in LATE[half].items()})
    return near


def sigmoid(v):
    return 0.5 * jnp.tanh(0.5 * v) + 0.5


def taps_of(row):
    lane = lax.broadcasted_iota(jnp.int32, row.shape, 1)
    zero = jnp.zeros_like(row)
    before = jnp.where(lane == 0, zero, pltpu.roll(row, 1, 1))
    after = jnp.where(lane == GW - 1, zero, pltpu.roll(row, GW - 1, 1))
    return jnp.concatenate([before, row, after], axis=0)


def accessors(ref, fields):
    core = ref["sc"][0]
    top = ref["sc"][1]
    first_core = core == 0

    def keep(row, value):
        if 0 <= row < OWN:
            return value
        g = top + row
        return jnp.where(jnp.logical_and(g >= 0, g < 128), value, jnp.zeros_like(value))

    def fetch(field, row):
        (own, slot), (near, near_at, far, far_at, count) = fields[field]
        if 0 <= row < OWN:
            return ref[own][slot, row]
        if row < 0:
            unit = count + row
            value = jnp.where(first_core, ref[far][far_at + unit], ref[near][near_at + unit])
        else:
            unit = row - OWN
            value = jnp.where(first_core, ref[near][near_at + unit], ref[far][far_at + unit])
        return keep(row, value)

    return first_core, keep, fetch


def stacked(bufs, q):
    cols = [
        jnp.concatenate([buf[i + a] for buf in bufs for a in range(3)], axis=0) for i in (q, q + 1)
    ]
    return jnp.concatenate(cols, axis=1)


def early_kernel(plan, *refs):
    names, half = plan["names"], plan["half"]
    ref = dict(zip(names, refs))
    sums, tx, th, th2 = refs[len(names) : len(names) + 2], *refs[len(names) + 2 :]
    _, _, fetch = accessors(ref, plan["fields"])
    filled = set()

    def fill(buf, field, reach, upto):
        for i in range(upto):
            if (field, i) not in filled:
                filled.add((field, i))
                buf[i] = taps_of(fetch(field, i - reach))

    for index in range(2):
        layer = plan["layer"] + index
        for q in range(0, OWN + 2 * REACH[index], 2):
            with_x = half == 0 and index == 0
            fill((th, th2)[index], ("HB", "HT")[index], REACH[index] + 1, q + 4)
            h = stacked([(th, th2)[index]], q)
            own = jnp.dot(ref["wa"][layer], h[0:512], preferred_element_type=F32)
            if with_x:
                fill(tx, "X", 4, q + 4)
                x = stacked([tx], q)
                shared = jnp.dot(
                    ref["wb"][layer, :, 0:640],
                    jnp.concatenate([x, h[512:576]], axis=0),
                    preferred_element_type=F32,
                )
                sums[index][q // 2, 0:256] = own + shared[0:256]
                sums[index][q // 2, 256:448] = shared[256:448]
            else:
                rest = jnp.concatenate([jnp.zeros((64, 2 * GW), BF), h[512:576]], axis=0)
                sums[index][q // 2] = own + jnp.dot(
                    ref["wb"][layer, 0:256, 512:640], rest, preferred_element_type=F32
                )


def phase_kernel(plan, *refs):
    names = plan["names"]
    outs = plan["outs"]
    n_in = len(names)
    ref = dict(zip(names, refs[:n_in]))
    out = dict(zip(outs, refs[n_in : n_in + len(outs)]))
    tx, th, tm, tx2, th2, tm2, yb, ob, yb2, ob2 = refs[n_in + len(outs) :]
    state_out = out["state"]
    first_core, keep, fetch = accessors(ref, plan["fields"])

    rows_of = [list(range(-reach, OWN + reach)) for reach in REACH]
    bufs = ((tx, th, tm, yb, ob), (tx2, th2, tm2.at[1:9], yb2, ob2))
    filled = set()

    def fill(buf, key, field, reach, upto):
        for i in range(upto):
            if (key, i) not in filled:
                filled.add((key, i))
                buf[i] = taps_of(fetch(field, i - reach))

    early = plan["early"]

    def matmuls(index, q):
        bx, bh, bm, _, _ = bufs[index]
        layer = plan["layer"] + index
        add = lambda w, rhs: jnp.dot(w, rhs, preferred_element_type=F32)
        if index == 0:
            fill(tm, "m", "M", 4, q + 4)
            if not (early and plan["half"] == 0):
                fill(tx, "x", "X", 4, q + 4)
        m = stacked([bm], q)
        rest = add(ref["wc"][layer], m[128:576])
        if early and plan["half"] == 0 and index == 0:
            acc2 = rest + add(ref["wb"][layer, 256:448, 640:768], m[0:128])
            return ref["sums0"][q // 2, 0:256], acc2 + ref["sums0"][q // 2, 256:448]
        if early:
            h_rest = jnp.zeros((64, 2 * GW), BF)
            own = ref[f"sums{index}"][q // 2]
        else:
            if index == 0:
                fill(th, "h", "HB", 4, q + 4)
            else:
                fill(th2, "h2", "HT", 2, q + 4)
            h = stacked([bh], q)
            h_rest = h[512:576]
            own = add(ref["wa"][layer], h[0:512])
        shared = add(
            ref["wb"][layer], jnp.concatenate([stacked([bx], q), h_rest, m[0:128]], axis=0)
        )
        return shared[0:256] + own, shared[256:448] + rest

    def gates(index, q, acc1, acc2):
        _, _, _, y_buf, o_buf = bufs[index]
        rows = rows_of[index]
        pair = (rows[q], rows[q + 1])
        c_field = "CT" if index else "CB"
        c_prev = jnp.concatenate([fetch(c_field, row) for row in pair], axis=1).astype(F32)
        if index:
            m_rows = [tm2[row + 3, 64:128] for row in pair]
        else:
            m_rows = [tm[row + 4, 64:128] for row in pair]
        m_prev = jnp.concatenate(m_rows, axis=1).astype(F32)
        c_new = sigmoid(acc1[64:128] + 1.0) * c_prev + sigmoid(acc1[0:64]) * jnp.tanh(acc1[128:192])
        m_new = sigmoid(acc2[64:128] + 1.0) * m_prev + sigmoid(acc2[0:64]) * jnp.tanh(acc2[128:192])
        c_new = c_new.astype(BF)
        m_new = m_new.astype(BF)
        lanes = slice(q * GW, (q + 2) * GW)
        o_buf[:, lanes] = acc1[192:256]
        blocks = []
        for j, row in enumerate(pair):
            c_row = keep(row, c_new[:, j * GW : (j + 1) * GW])
            m_row = keep(row, m_new[:, j * GW : (j + 1) * GW])
            if 0 <= row < OWN:
                state_out[SLOT[c_field], row] = c_row
                if index:
                    state_out[SLOT["M"], row] = m_row
            c_taps = taps_of(c_row)
            m_taps = taps_of(m_row)
            if not index:
                tm2[row + 3] = m_taps
            blocks.append(
                jnp.concatenate(
                    [t[64 * b : 64 * b + 64] for b in range(3) for t in (c_taps, m_taps)], axis=0
                )
            )
        y_buf[:, lanes] = jnp.dot(
            ref["wo"][plan["layer"] + index],
            jnp.concatenate(blocks, axis=1),
            preferred_element_type=F32,
        )

    def hidden(index, q):
        _, _, _, y_buf, o_buf = bufs[index]
        lanes = slice(q * GW, (q + 1) * GW)
        gate = (
            o_buf[:, lanes]
            + y_buf[0:64, (q - 1) * GW : q * GW]
            + y_buf[64:128, lanes]
            + y_buf[128:192, (q + 1) * GW : (q + 2) * GW]
        )
        h_new = (sigmoid(gate) * jnp.tanh(y_buf[192:256, lanes])).astype(BF)
        row = rows_of[index][q]
        h_new = keep(row, h_new)
        if 0 <= row < OWN:
            state_out[SLOT["HT" if index else "HB"], row] = h_new
        if not index:
            tx2[row + 2] = taps_of(h_new)

    def finish(index, q, accs):
        gates(index, q, *accs)
        for h in (q - 1, q):
            if h >= 1:
                hidden(index, h)

    tasks = [(i, q) for i in range(2) for q in range(0, len(rows_of[i]), 2)]
    waiting = None
    for task in tasks:
        accs = matmuls(*task)
        if waiting is not None:
            finish(*waiting)
        waiting = task + (accs,)
    finish(*waiting)

    def send(target, layout, last_rows_if):
        for field, (offset, count) in layout.items():
            for u in range(count):
                low = state_out[SLOT[field], u]
                high = state_out[SLOT[field], OWN - count + u]
                target[offset + u] = jnp.where(last_rows_if, high, low)

    half = plan["half"]
    if "give" in out:
        lower, slots = ref[plan["lower"]], out["give"].shape[0]
        for slot in range(slots):
            for row in range(OWN):
                out["give"][slot, row] = jnp.where(
                    first_core, state_out[slot, row], lower[slot, row]
                )
    if "near" in out:
        send(out["near"], both(half) if "late" in out else SOON[half], first_core)
    if "soon" in out:
        send(out["soon"], SOON[half], jnp.logical_not(first_core))
    if "late" in out:
        send(out["late"], LATE[half], jnp.logical_not(first_core))


def run_early(operands, plan):
    names = list(operands)
    plan = dict(plan, names=names)
    height = 448 if plan["half"] == 0 else 256
    taps = (3 * CH, GW)
    return pl.pallas_call(
        functools.partial(early_kernel, plan),
        out_shape=[
            jax.ShapeDtypeStruct((5, height, 2 * GW), F32),
            jax.ShapeDtypeStruct((3, 256, 2 * GW), F32),
        ],
        in_specs=[
            pl.BlockSpec(memory_space=pltpu.SMEM if name == "sc" else pltpu.VMEM) for name in names
        ],
        out_specs=[pl.BlockSpec(memory_space=pltpu.VMEM)] * 2,
        scratch_shapes=[
            pltpu.VMEM((12,) + taps, BF), pltpu.VMEM((12,) + taps, BF), pltpu.VMEM((8,) + taps, BF)
        ],
        compiler_params=pltpu.CompilerParams(vmem_limit_bytes=12 << 20),
        name="early_sums",
    )(*[operands[name] for name in names])


def run_phase(operands, plan):
    names = list(operands)
    plan = dict(plan, names=names)
    unit = (CH, GW)
    half = plan["half"]
    sizes = {"state": (5, OWN) + unit}
    if plan["send"]:
        far = {"soon": units(SOON[half])}
        if plan["send"] > 1:
            far["late"] = units(LATE[half])
        sizes["near"] = (sum(far.values()),) + unit
        sizes.update({k: (n,) + unit for k, n in far.items()})
    else:
        sizes["give"] = sizes["state"]
    plan["outs"] = list(sizes)
    in_specs = [
        pl.BlockSpec(memory_space=pltpu.SMEM if name == "sc" else pltpu.VMEM) for name in names
    ]
    results = pl.pallas_call(
        functools.partial(phase_kernel, plan),
        out_shape=[jax.ShapeDtypeStruct(s, BF) for s in sizes.values()],
        in_specs=in_specs,
        out_specs=[pl.BlockSpec(memory_space=pltpu.VMEM) for _ in sizes],
        scratch_shapes=[
            pltpu.VMEM((12, 3 * CH, GW), BF),
            pltpu.VMEM((12, 3 * CH, GW), BF),
            pltpu.VMEM((12, 3 * CH, GW), BF),
            pltpu.VMEM((8, 3 * CH, GW), BF),
            pltpu.VMEM((8, 3 * CH, GW), BF),
            pltpu.VMEM((10, 3 * CH, GW), BF),
            pltpu.VMEM((4 * CH, 10 * GW), F32),
            pltpu.VMEM((CH, 10 * GW), F32),
            pltpu.VMEM((4 * CH, 6 * GW), F32),
            pltpu.VMEM((CH, 6 * GW), F32),
        ],
        compiler_params=pltpu.CompilerParams(vmem_limit_bytes=24 << 20),
        name="two_layers",
    )(*[operands[name] for name in names])
    return dict(zip(sizes, results))


def in_hbm(*values):
    return [pltpu.with_memory_space_constraint(v, pltpu.HBM) for v in values]


def pack_weights_kernel(sc, *refs):
    sources, (wa, wb, wc, wo) = refs[:10], refs[10:14]
    inputs, sems = refs[14:24], refs[24]
    core = sc[0]
    copies = [pltpu.make_async_copy(s, t, sems.at[i]) for i, (s, t) in enumerate(zip(sources, inputs))]
    for c in copies:
        c.start()
    for group in range(2):
        for c in copies[5 * group : 5 * group + 5]:
            c.wait()
        x, h, m, o, last = inputs[5 * group : 5 * group + 5]
        first = 2 * core if group == 0 else 2 - 2 * core
        for l in range(2):
            at = first + l
            xt = x[l]
            ht = jnp.transpose(h[l])
            mt = m[l]
            ot = o[l]
            wa[at] = ht[:, 0:512]
            wc[at] = mt[:, 128:576]
            gate_rows = jnp.concatenate([xt[0:192], xt[384:448]], axis=0)
            wb[at, 0:256, 0:512] = gate_rows[:, 0:512]
            wb[at, 0:256, 512:640] = jnp.concatenate([gate_rows[:, 512:576], ht[:, 512:576]], axis=1)
            wb[at, 0:256, 640:768] = jnp.zeros((256, 128), BF)
            wb[at, 256:448, 0:512] = xt[192:384, 0:512]
            wb[at, 256:448, 512:640] = jnp.concatenate(
                [xt[192:384, 512:576], jnp.zeros((192, 64), BF)], axis=1
            )
            wb[at, 256:448, 640:768] = mt[:, 0:128]
            for a in range(3):
                wo[at, 64 * a : 64 * a + 64] = ot[:, 384 * a : 384 * a + 384]
            wo[at, 192:256, 0:128] = jnp.zeros((64, 128), BF)
            wo[at, 192:256, 128:256] = last[l]
            wo[at, 192:256, 256:384] = jnp.zeros((64, 128), BF)


def pack_weights(scalars, own, other):
    shapes = ((4, 256, 512), (4, 448, 768), (4, 192, 448), (4, 256, 384))
    vmem = pl.BlockSpec(memory_space=pltpu.VMEM)
    return pl.pallas_call(
        pack_weights_kernel,
        out_shape=[jax.ShapeDtypeStruct(s, BF) for s in shapes],
        in_specs=[pl.BlockSpec(memory_space=pltpu.SMEM)]
        + [pl.BlockSpec(memory_space=pltpu.HBM)] * 10,
        out_specs=[vmem] * 4,
        scratch_shapes=[pltpu.VMEM(w.shape, BF) for w in (*own, *other)]
        + [pltpu.SemaphoreType.DMA((10,))],
        compiler_params=pltpu.CompilerParams(vmem_limit_bytes=32 << 20),
        name="pack_weights",
    )(scalars, *in_hbm(*own), *other)


def cut_state_kernel(sc, *refs):
    sources, pieces, copied, sems = refs[:4], refs[4:8], refs[8:12], refs[12]
    copies = [pltpu.make_async_copy(s, t, sems.at[i]) for i, (s, t) in enumerate(zip(sources, copied))]
    for c in copies:
        c.start()
    for c in copies:
        c.wait()
    frames, hidden, cell, memory = copied
    first_core, z = sc[0] == 0, sc[2]
    for k in range(4):
        seq = lax.rem(z + k, 4)
        for i in range(2):
            for l in range(2):
                pieces[k][l, i] = hidden[l, seq, i]
                pieces[k][2 + l, i] = cell[l, seq, i]
            pieces[k][4, i] = jnp.where(first_core, memory[seq, i], frames[1, seq, i])
            pieces[k][5, i] = jnp.where(first_core, frames[0, seq, i], frames[2, seq, i])


def cut_state(scalars, frames, hidden, cell, memory):
    vmem = pl.BlockSpec(memory_space=pltpu.VMEM)
    return pl.pallas_call(
        cut_state_kernel,
        out_shape=[jax.ShapeDtypeStruct((6, 2, CH, GW), BF)] * 4,
        in_specs=[pl.BlockSpec(memory_space=pltpu.SMEM)]
        + [pl.BlockSpec(memory_space=pltpu.HBM)] * 4,
        out_specs=[vmem] * 4,
        scratch_shapes=[pltpu.VMEM(v.shape, BF) for v in (frames, hidden, cell, memory)]
        + [pltpu.SemaphoreType.DMA((4,))],
        compiler_params=pltpu.CompilerParams(vmem_limit_bytes=8 << 20),
        name="cut_state",
    )(scalars, *in_hbm(frames, hidden, cell, memory))


ORDER_A = ((1, "HT"), (4, "M"), (0, "HB"), (2, "CB"), (3, "CT"), (5, "F0"))
ORDER_B = ((1, "HT"), (0, "HB"), (2, "CB"), (3, "CT"), (4, "F1"), (5, "F2"))


def open_state_kernel(sc, *refs):
    mine, theirs = refs[:4], refs[4:8]
    low_own, high_own, near_a, near_b, far_a, far_b, rows = refs[8:]
    core, z = sc[0], sc[2]
    for k in range(4):
        at = 2 * lax.rem(z + 4 - k, 4)
        for i in range(2):
            for a in range(6):
                rows[0, a, at + i] = mine[k][a, i]
                rows[1, a, at + i] = theirs[k][a, i]
    other = 1 - core
    for a in range(6):
        for r in range(OWN):
            low_own[a, r] = rows[core, a, 4 * core + r]
            high_own[a, r] = rows[other, a, 4 * core + r]
    for group, order, layout, near, far in (
        (core, ORDER_A, FIRST_A, near_a, far_a),
        (other, ORDER_B, FIRST_B, near_b, far_b),
    ):
        for a, name in order:
            offset, count = layout[name]
            for u in range(count):
                turn = core * (OWN - count) + u
                far[offset + u] = rows[group, a, 4 * core + turn]
                near[offset + u] = rows[group, a, 4 * other + turn]


def open_state(scalars, mine, theirs):
    vmem = pl.BlockSpec(memory_space=pltpu.VMEM)
    shapes = [(6, OWN)] * 2 + [(18,)] * 4
    return pl.pallas_call(
        open_state_kernel,
        out_shape=[jax.ShapeDtypeStruct(s + (CH, GW), BF) for s in shapes],
        in_specs=[pl.BlockSpec(memory_space=pltpu.SMEM)] + [vmem] * 8,
        out_specs=[vmem] * 6,
        scratch_shapes=[pltpu.VMEM((2, 6, 8, CH, GW), BF)],
        compiler_params=pltpu.CompilerParams(vmem_limit_bytes=16 << 20),
        name="open_state",
    )(scalars, *mine, *theirs)


def cut_result_kernel(sc, low, high, taken, *pieces):
    core, z = sc[0], sc[2]
    for k in range(4):
        to = lax.rem(z + k, 4)
        here = (to // 2) == core
        row = 2 * lax.rem(to, 2)
        for a in range(5):
            for i in range(2):
                own = jnp.where(core == 0, low[a, row + i], high[a, row + i])
                pieces[k][a, i] = jnp.where(here, own, taken[a, row + i])


def cut_result(scalars, low, high, taken):
    vmem = pl.BlockSpec(memory_space=pltpu.VMEM)
    return pl.pallas_call(
        cut_result_kernel,
        out_shape=[jax.ShapeDtypeStruct((5, 2, CH, GW), BF)] * 4,
        in_specs=[pl.BlockSpec(memory_space=pltpu.SMEM)] + [vmem] * 3,
        out_specs=[vmem] * 4,
        compiler_params=pltpu.CompilerParams(vmem_limit_bytes=8 << 20),
        name="cut_result",
    )(scalars, low, high, taken)


def close_result_kernel(sc, *refs):
    parts = refs[:4]
    hidden, cell, memory = refs[4:]
    z = sc[2]
    for k in range(4):
        seq = lax.rem(z + 4 - k, 4)
        for i in range(2):
            for a in range(2):
                hidden[a, seq, i] = parts[k][a, i]
                cell[a, seq, i] = parts[k][2 + a, i]
            memory[0, seq, i] = parts[k][4, i]


def close_result(scalars, parts):
    vmem = pl.BlockSpec(memory_space=pltpu.VMEM)
    shapes = ((2, 4, 2), (2, 4, 2), (1, 4, 2))
    return pl.pallas_call(
        close_result_kernel,
        out_shape=[jax.ShapeDtypeStruct(s + (CH, GW), BF) for s in shapes],
        in_specs=[pl.BlockSpec(memory_space=pltpu.SMEM)] + [vmem] * 4,
        out_specs=[vmem] * 3,
        compiler_params=pltpu.CompilerParams(vmem_limit_bytes=8 << 20),
        name="close_result",
    )(scalars, *parts)


def program(frames, hidden_in, cell_in, memory_in, w_x, w_h, w_m, w_o, w_last):
    core = lax.axis_index("layer")
    chip = lax.axis_index("rows")
    chips = lax.axis_size("rows")
    swap = [(0, 1), (1, 0)]
    across = []
    for i in range(chips):
        across.append((chips + i, i + 4 if i + 4 < chips else chips + (i ^ 1)))
        across.append((i, chips + i - 4 if i >= 4 else i ^ 1))

    def to_partner(value):
        return lax.ppermute(value, "layer", swap)

    def to_neighbour(value):
        return lax.ppermute(value, ("layer", "rows"), across)

    def around(value, k):
        turn = [(i, 4 * (i // 4) + (i + k) % 4) for i in range(chips)]
        return lax.ppermute(value, "rows", turn)

    scalars = jnp.stack([core, 8 * (chip // 4) + 4 * core, chip % 4]).astype(jnp.int32)
    turned = [jnp.swapaxes(w, 1, 2) for w in (w_x, w_m, w_o, w_last)]
    scalars, own_w = lax.optimization_barrier(
        (scalars, [turned[0], w_h, turned[1], turned[2], turned[3]])
    )
    other_w = [to_partner(w) for w in own_w]
    wa, wb, wc, wo = pack_weights(scalars, own_w, other_w)

    pieces = cut_state(scalars, frames, hidden_in, cell_in, memory_in)
    mine = [pieces[0]] + [around(pieces[k], k) for k in (1, 2, 3)]
    theirs = [to_partner(piece) for piece in mine]
    low_own, high_own, near_a, near_b, message_a, message_b = open_state(scalars, mine, theirs)
    far_a = to_neighbour(message_a)
    far_b = to_neighbour(message_b)

    base = {"sc": scalars, "wa": wa, "wb": wb, "wc": wc, "wo": wo}
    arrays = {"s00": low_own, "s01": high_own, "na": near_a, "fa": far_a, "nb": near_b, "fb": far_b}

    def first(letter, layout, field):
        offset, count = layout[field]
        return ("n" + letter, offset, "f" + letter, offset, count)

    kept = ("HB", "HT", "CB", "CT")
    halo = [{k: first("a", FIRST_A, k) for k in kept}, {k: first("b", FIRST_B, k) for k in kept}]
    states = ["s00", "s01"]
    own_m = ("s00", 4)
    halo_m = first("a", FIRST_A, "M")
    frame_field = (
        (("s00", 5), first("a", FIRST_A, "F0")),
        (("s01", 4), first("b", FIRST_B, "F1")),
        (("s01", 5), first("b", FIRST_B, "F2")),
    )
    steps = frames.shape[0]
    results = [None, None]
    for step in range(steps):
        x_field = frame_field[step]
        for half in range(2):
            send = 2 if step < steps - 1 else 1 - half
            fields = {k: ((states[half], SLOT[k]), halo[half][k]) for k in kept}
            fields["M"] = (own_m, halo_m)
            fields["X"] = x_field
            tag = f"{step}{half}"
            early = tag != "00"
            ahead = ("HB", "HT", "X") if half == 0 else ("HB", "HT")

            def gather(wanted, weights):
                used = {k: fields[k] for k in wanted}
                needed = {f[0][0] for f in used.values()}
                needed |= {f[1][i] for f in used.values() for i in (0, 2)}
                operands = {k: base[k] for k in ("sc",) + weights}
                operands.update({name: arrays[name] for name in sorted(needed)})
                return used, operands

            plan = {"half": half, "layer": 2 * half, "send": send, "early": early}
            if early:
                used, operands = gather(ahead, ("wa", "wb"))
                sums = run_early(operands, dict(plan, fields=used))
                used, operands = gather(
                    [k for k in fields if k not in ahead], ("wb", "wc", "wo")
                )
                operands.update(sums0=sums[0], sums1=sums[1])
            else:
                used, operands = gather(fields, ("wa", "wb", "wc", "wo"))
            plan["fields"] = used
            if not send:
                plan["lower"] = states[0]
                operands[states[0]] = arrays[states[0]]
            outs = run_phase(operands, plan)
            results[half] = outs["state"]
            states[half] = "state" + tag
            arrays["state" + tag] = outs["state"]
            own_m = ("state" + tag, SLOT["M"])
            if send:
                arrays["soon" + tag] = to_neighbour(outs["soon"])
                arrays["near" + tag] = to_partner(outs["near"])
                near_at = both(half)
                for k, (o, n) in SOON[half].items():
                    spec = ("near" + tag, near_at[k][0], "soon" + tag, o, n)
                    if k == "M":
                        halo_m = spec
                    else:
                        x_field = (("state" + tag, SLOT["HT"]), spec)
                        halo[half][k] = spec
            if send > 1:
                arrays["late" + tag] = to_neighbour(outs["late"])
                for k, (o, n) in LATE[half].items():
                    halo[half][k] = ("near" + tag, near_at[k][0], "late" + tag, o, n)

    taken = to_partner(outs["give"])
    pieces = cut_result(scalars, results[0], results[1], taken)
    done = [pieces[0]] + [around(pieces[k], k) for k in (1, 2, 3)]
    return tuple(close_result(scalars, done))


def solution(mesh):
    return jax.shard_map(
        program,
        mesh=mesh,
        in_specs=(
            P(None, None, "rows", None, None),
            P("layer", None, "rows", None, None),
            P("layer", None, "rows", None, None),
            P(None, "rows", None, None),
            P("layer", None, None),
            P("layer", None, None),
            P("layer", None, None),
            P("layer", None, None),
            P("layer", None, None),
        ),
        out_specs=(
            P("layer", None, "rows", None, None),
            P("layer", None, "rows", None, None),
            P("layer", None, "rows", None, None),
        ),
        check_vma=False,
    )
```

```python
import functools

import jax
import jax.numpy as jnp
from jax import lax
from jax.experimental import pallas as pl
from jax.experimental.pallas import tpu as pltpu
from jax.sharding import PartitionSpec as P


CH = 64
GW = 128
OWN = 4
BF = jnp.bfloat16
F32 = jnp.float32

FIRST_A = {"HT": (0, 2), "M": (2, 4), "HB": (6, 4), "CB": (10, 3), "CT": (13, 1), "F0": (14, 4)}
FIRST_B = {"HT": (0, 2), "HB": (2, 4), "CB": (6, 3), "CT": (9, 1), "F1": (10, 4), "F2": (14, 4)}
SOON = ({"HT": (0, 4), "M": (4, 4)}, {"M": (0, 4)})
LATE = (
    {"HB": (0, 4), "CB": (4, 3), "CT": (7, 1)},
    {"HT": (0, 2), "HB": (2, 4), "CB": (6, 3), "CT": (9, 1)},
)
SLOT = {"HB": 0, "HT": 1, "CB": 2, "CT": 3, "M": 4}
REACH = (3, 1)


def units(layout):
    return sum(count for _, count in layout.values())


def both(half):
    shift = units(SOON[half])
    near = dict(SOON[half])
    near.update({k: (o + shift, n) for k, (o, n) in LATE[half].items()})
    return near


def sigmoid(v):
    return 0.5 * jnp.tanh(0.5 * v) + 0.5


def taps_of(row):
    lane = lax.broadcasted_iota(jnp.int32, row.shape, 1)
    zero = jnp.zeros_like(row)
    before = jnp.where(lane == 0, zero, pltpu.roll(row, 1, 1))
    after = jnp.where(lane == GW - 1, zero, pltpu.roll(row, GW - 1, 1))
    return jnp.concatenate([before, row, after], axis=0)


def accessors(ref, fields):
    core = ref["sc"][0]
    top = ref["sc"][1]
    first_core = core == 0

    def keep(row, value):
        if 0 <= row < OWN:
            return value
        g = top + row
        return jnp.where(jnp.logical_and(g >= 0, g < 128), value, jnp.zeros_like(value))

    def fetch(field, row):
        (own, slot), (near, near_at, far, far_at, count) = fields[field]
        if 0 <= row < OWN:
            return ref[own][slot, row]
        if row < 0:
            unit = count + row
            value = jnp.where(first_core, ref[far][far_at + unit], ref[near][near_at + unit])
        else:
            unit = row - OWN
            value = jnp.where(first_core, ref[near][near_at + unit], ref[far][far_at + unit])
        return keep(row, value)

    return first_core, keep, fetch


def stacked(bufs, q):
    cols = [
        jnp.concatenate([buf[i + a] for buf in bufs for a in range(3)], axis=0) for i in (q, q + 1)
    ]
    return jnp.concatenate(cols, axis=1)


def early_kernel(plan, *refs):
    names, half = plan["names"], plan["half"]
    ref = dict(zip(names, refs))
    sums, tx, th, th2 = refs[len(names) : len(names) + 2], *refs[len(names) + 2 :]
    _, _, fetch = accessors(ref, plan["fields"])
    filled = set()

    def fill(buf, field, reach, upto):
        for i in range(upto):
            if (field, i) not in filled:
                filled.add((field, i))
                buf[i] = taps_of(fetch(field, i - reach))

    for index in range(2):
        layer = plan["layer"] + index
        for q in range(0, OWN + 2 * REACH[index], 2):
            with_x = half == 0 and index == 0
            fill((th, th2)[index], ("HB", "HT")[index], REACH[index] + 1, q + 4)
            h = stacked([(th, th2)[index]], q)
            own = jnp.dot(ref["wa"][layer], h[0:512], preferred_element_type=F32)
            if with_x:
                fill(tx, "X", 4, q + 4)
                x = stacked([tx], q)
                shared = jnp.dot(
                    ref["wb"][layer, :, 0:640],
                    jnp.concatenate([x, h[512:576]], axis=0),
                    preferred_element_type=F32,
                )
                sums[index][q // 2, 0:256] = own + shared[0:256]
                sums[index][q // 2, 256:448] = shared[256:448]
            else:
                rest = jnp.concatenate([jnp.zeros((64, 2 * GW), BF), h[512:576]], axis=0)
                sums[index][q // 2] = own + jnp.dot(
                    ref["wb"][layer, 0:256, 512:640], rest, preferred_element_type=F32
                )


def phase_kernel(plan, *refs):
    names = plan["names"]
    outs = plan["outs"]
    n_in = len(names)
    ref = dict(zip(names, refs[:n_in]))
    out = dict(zip(outs, refs[n_in : n_in + len(outs)]))
    tx, th, tm, tx2, th2, tm2, yb, ob, yb2, ob2 = refs[n_in + len(outs) :]
    state_out = out["state"]
    first_core, keep, fetch = accessors(ref, plan["fields"])

    rows_of = [list(range(-reach, OWN + reach)) for reach in REACH]
    bufs = ((tx, th, tm, yb, ob), (tx2, th2, tm2.at[1:9], yb2, ob2))
    filled = set()

    def fill(buf, key, field, reach, upto):
        for i in range(upto):
            if (key, i) not in filled:
                filled.add((key, i))
                buf[i] = taps_of(fetch(field, i - reach))

    early = plan["early"]

    def matmuls(index, q):
        bx, bh, bm, _, _ = bufs[index]
        layer = plan["layer"] + index
        add = lambda w, rhs: jnp.dot(w, rhs, preferred_element_type=F32)
        if index == 0:
            fill(tm, "m", "M", 4, q + 4)
            if not (early and plan["half"] == 0):
                fill(tx, "x", "X", 4, q + 4)
        m = stacked([bm], q)
        rest = add(ref["wc"][layer], m[128:576])
        if early and plan["half"] == 0 and index == 0:
            acc2 = rest + add(ref["wb"][layer, 256:448, 640:768], m[0:128])
            return ref["sums0"][q // 2, 0:256], acc2 + ref["sums0"][q // 2, 256:448]
        if early:
            h_rest = jnp.zeros((64, 2 * GW), BF)
            own = ref[f"sums{index}"][q // 2]
        else:
            if index == 0:
                fill(th, "h", "HB", 4, q + 4)
            else:
                fill(th2, "h2", "HT", 2, q + 4)
            h = stacked([bh], q)
            h_rest = h[512:576]
            own = add(ref["wa"][layer], h[0:512])
        shared = add(
            ref["wb"][layer], jnp.concatenate([stacked([bx], q), h_rest, m[0:128]], axis=0)
        )
        return shared[0:256] + own, shared[256:448] + rest

    def gates(index, q, acc1, acc2):
        _, _, _, y_buf, o_buf = bufs[index]
        rows = rows_of[index]
        pair = (rows[q], rows[q + 1])
        c_field = "CT" if index else "CB"
        c_prev = jnp.concatenate([fetch(c_field, row) for row in pair], axis=1).astype(F32)
        if index:
            m_rows = [tm2[row + 3, 64:128] for row in pair]
        else:
            m_rows = [tm[row + 4, 64:128] for row in pair]
        m_prev = jnp.concatenate(m_rows, axis=1).astype(F32)
        c_new = sigmoid(acc1[64:128] + 1.0) * c_prev + sigmoid(acc1[0:64]) * jnp.tanh(acc1[128:192])
        m_new = sigmoid(acc2[64:128] + 1.0) * m_prev + sigmoid(acc2[0:64]) * jnp.tanh(acc2[128:192])
        c_new = c_new.astype(BF)
        m_new = m_new.astype(BF)
        lanes = slice(q * GW, (q + 2) * GW)
        o_buf[:, lanes] = acc1[192:256]
        blocks = []
        for j, row in enumerate(pair):
            c_row = keep(row, c_new[:, j * GW : (j + 1) * GW])
            m_row = keep(row, m_new[:, j * GW : (j + 1) * GW])
            if 0 <= row < OWN:
                state_out[SLOT[c_field], row] = c_row
                if index:
                    state_out[SLOT["M"], row] = m_row
            c_taps = taps_of(c_row)
            m_taps = taps_of(m_row)
            if not index:
                tm2[row + 3] = m_taps
            blocks.append(
                jnp.concatenate(
                    [t[64 * b : 64 * b + 64] for b in range(3) for t in (c_taps, m_taps)], axis=0
                )
            )
        y_buf[:, lanes] = jnp.dot(
            ref["wo"][plan["layer"] + index],
            jnp.concatenate(blocks, axis=1),
            preferred_element_type=F32,
        )

    def hidden(index, q):
        _, _, _, y_buf, o_buf = bufs[index]
        lanes = slice(q * GW, (q + 1) * GW)
        gate = (
            o_buf[:, lanes]
            + y_buf[0:64, (q - 1) * GW : q * GW]
            + y_buf[64:128, lanes]
            + y_buf[128:192, (q + 1) * GW : (q + 2) * GW]
        )
        h_new = (sigmoid(gate) * jnp.tanh(y_buf[192:256, lanes])).astype(BF)
        row = rows_of[index][q]
        h_new = keep(row, h_new)
        if 0 <= row < OWN:
            state_out[SLOT["HT" if index else "HB"], row] = h_new
        if not index:
            tx2[row + 2] = taps_of(h_new)

    def finish(index, q, accs):
        gates(index, q, *accs)
        for h in (q - 1, q):
            if h >= 1:
                hidden(index, h)

    tasks = [(i, q) for i in range(2) for q in range(0, len(rows_of[i]), 2)]
    waiting = None
    for task in tasks:
        accs = matmuls(*task)
        if waiting is not None:
            finish(*waiting)
        waiting = task + (accs,)
    finish(*waiting)

    def send(target, layout, last_rows_if):
        for field, (offset, count) in layout.items():
            for u in range(count):
                low = state_out[SLOT[field], u]
                high = state_out[SLOT[field], OWN - count + u]
                target[offset + u] = jnp.where(last_rows_if, high, low)

    half = plan["half"]
    if "give" in out:
        lower, slots = ref[plan["lower"]], out["give"].shape[0]
        for slot in range(slots):
            for row in range(OWN):
                out["give"][slot, row] = jnp.where(
                    first_core, state_out[slot, row], lower[slot, row]
                )
    if "near" in out:
        send(out["near"], both(half) if "late" in out else SOON[half], first_core)
    if "soon" in out:
        send(out["soon"], SOON[half], jnp.logical_not(first_core))
    if "late" in out:
        send(out["late"], LATE[half], jnp.logical_not(first_core))


def run_early(operands, plan):
    names = list(operands)
    plan = dict(plan, names=names)
    height = 448 if plan["half"] == 0 else 256
    taps = (3 * CH, GW)
    return pl.pallas_call(
        functools.partial(early_kernel, plan),
        out_shape=[
            jax.ShapeDtypeStruct((5, height, 2 * GW), F32),
            jax.ShapeDtypeStruct((3, 256, 2 * GW), F32),
        ],
        in_specs=[
            pl.BlockSpec(memory_space=pltpu.SMEM if name == "sc" else pltpu.VMEM) for name in names
        ],
        out_specs=[pl.BlockSpec(memory_space=pltpu.VMEM)] * 2,
        scratch_shapes=[
            pltpu.VMEM((12,) + taps, BF), pltpu.VMEM((12,) + taps, BF), pltpu.VMEM((8,) + taps, BF)
        ],
        compiler_params=pltpu.CompilerParams(vmem_limit_bytes=12 << 20),
        name="early_sums",
    )(*[operands[name] for name in names])


def run_phase(operands, plan):
    names = list(operands)
    plan = dict(plan, names=names)
    unit = (CH, GW)
    half = plan["half"]
    sizes = {"state": (5, OWN) + unit}
    if plan["send"]:
        far = {"soon": units(SOON[half])}
        if plan["send"] > 1:
            far["late"] = units(LATE[half])
        sizes["near"] = (sum(far.values()),) + unit
        sizes.update({k: (n,) + unit for k, n in far.items()})
    else:
        sizes["give"] = sizes["state"]
    plan["outs"] = list(sizes)
    in_specs = [
        pl.BlockSpec(memory_space=pltpu.SMEM if name == "sc" else pltpu.VMEM) for name in names
    ]
    results = pl.pallas_call(
        functools.partial(phase_kernel, plan),
        out_shape=[jax.ShapeDtypeStruct(s, BF) for s in sizes.values()],
        in_specs=in_specs,
        out_specs=[pl.BlockSpec(memory_space=pltpu.VMEM) for _ in sizes],
        scratch_shapes=[
            pltpu.VMEM((12, 3 * CH, GW), BF),
            pltpu.VMEM((12, 3 * CH, GW), BF),
            pltpu.VMEM((12, 3 * CH, GW), BF),
            pltpu.VMEM((8, 3 * CH, GW), BF),
            pltpu.VMEM((8, 3 * CH, GW), BF),
            pltpu.VMEM((10, 3 * CH, GW), BF),
            pltpu.VMEM((4 * CH, 10 * GW), F32),
            pltpu.VMEM((CH, 10 * GW), F32),
            pltpu.VMEM((4 * CH, 6 * GW), F32),
            pltpu.VMEM((CH, 6 * GW), F32),
        ],
        compiler_params=pltpu.CompilerParams(vmem_limit_bytes=24 << 20),
        name="two_layers",
    )(*[operands[name] for name in names])
    return dict(zip(sizes, results))


def in_hbm(*values):
    return [pltpu.with_memory_space_constraint(v, pltpu.HBM) for v in values]


def pack_weights_kernel(sc, *refs):
    sources, (wa, wb, wc, wo) = refs[:10], refs[10:14]
    inputs, sems = refs[14:24], refs[24]
    core = sc[0]
    copies = [pltpu.make_async_copy(s, t, sems.at[i]) for i, (s, t) in enumerate(zip(sources, inputs))]
    for c in copies:
        c.start()
    for group in range(2):
        for c in copies[5 * group : 5 * group + 5]:
            c.wait()
        x, h, m, o, last = inputs[5 * group : 5 * group + 5]
        first = 2 * core if group == 0 else 2 - 2 * core
        for l in range(2):
            at = first + l
            xt = x[l]
            ht = jnp.transpose(h[l])
            mt = m[l]
            ot = o[l]
            wa[at] = ht[:, 0:512]
            wc[at] = mt[:, 128:576]
            gate_rows = jnp.concatenate([xt[0:192], xt[384:448]], axis=0)
            wb[at, 0:256, 0:512] = gate_rows[:, 0:512]
            wb[at, 0:256, 512:640] = jnp.concatenate([gate_rows[:, 512:576], ht[:, 512:576]], axis=1)
            wb[at, 0:256, 640:768] = jnp.zeros((256, 128), BF)
            wb[at, 256:448, 0:512] = xt[192:384, 0:512]
            wb[at, 256:448, 512:640] = jnp.concatenate(
                [xt[192:384, 512:576], jnp.zeros((192, 64), BF)], axis=1
            )
            wb[at, 256:448, 640:768] = mt[:, 0:128]
            for a in range(3):
                wo[at, 64 * a : 64 * a + 64] = ot[:, 384 * a : 384 * a + 384]
            wo[at, 192:256, 0:128] = jnp.zeros((64, 128), BF)
            wo[at, 192:256, 128:256] = last[l]
            wo[at, 192:256, 256:384] = jnp.zeros((64, 128), BF)


def pack_weights(scalars, own, other):
    shapes = ((4, 256, 512), (4, 448, 768), (4, 192, 448), (4, 256, 384))
    vmem = pl.BlockSpec(memory_space=pltpu.VMEM)
    return pl.pallas_call(
        pack_weights_kernel,
        out_shape=[jax.ShapeDtypeStruct(s, BF) for s in shapes],
        in_specs=[pl.BlockSpec(memory_space=pltpu.SMEM)]
        + [pl.BlockSpec(memory_space=pltpu.HBM)] * 10,
        out_specs=[vmem] * 4,
        scratch_shapes=[pltpu.VMEM(w.shape, BF) for w in (*own, *other)]
        + [pltpu.SemaphoreType.DMA((10,))],
        compiler_params=pltpu.CompilerParams(vmem_limit_bytes=32 << 20),
        name="pack_weights",
    )(scalars, *in_hbm(*own), *other)


def cut_state_kernel(sc, *refs):
    sources, pieces, copied, sems = refs[:4], refs[4:8], refs[8:12], refs[12]
    copies = [pltpu.make_async_copy(s, t, sems.at[i]) for i, (s, t) in enumerate(zip(sources, copied))]
    for c in copies:
        c.start()
    for c in copies:
        c.wait()
    frames, hidden, cell, memory = copied
    first_core, z = sc[0] == 0, sc[2]
    for k in range(4):
        seq = lax.rem(z + k, 4)
        for i in range(2):
            for l in range(2):
                pieces[k][l, i] = hidden[l, seq, i]
                pieces[k][2 + l, i] = cell[l, seq, i]
            pieces[k][4, i] = jnp.where(first_core, memory[seq, i], frames[1, seq, i])
            pieces[k][5, i] = jnp.where(first_core, frames[0, seq, i], frames[2, seq, i])


def cut_state(scalars, frames, hidden, cell, memory):
    vmem = pl.BlockSpec(memory_space=pltpu.VMEM)
    return pl.pallas_call(
        cut_state_kernel,
        out_shape=[jax.ShapeDtypeStruct((6, 2, CH, GW), BF)] * 4,
        in_specs=[pl.BlockSpec(memory_space=pltpu.SMEM)]
        + [pl.BlockSpec(memory_space=pltpu.HBM)] * 4,
        out_specs=[vmem] * 4,
        scratch_shapes=[pltpu.VMEM(v.shape, BF) for v in (frames, hidden, cell, memory)]
        + [pltpu.SemaphoreType.DMA((4,))],
        compiler_params=pltpu.CompilerParams(vmem_limit_bytes=8 << 20),
        name="cut_state",
    )(scalars, *in_hbm(frames, hidden, cell, memory))


ORDER_A = ((1, "HT"), (4, "M"), (0, "HB"), (2, "CB"), (3, "CT"), (5, "F0"))
ORDER_B = ((1, "HT"), (0, "HB"), (2, "CB"), (3, "CT"), (4, "F1"), (5, "F2"))


def open_state_kernel(sc, *refs):
    mine, theirs = refs[:4], refs[4:8]
    low_own, high_own, near_a, near_b, far_a, far_b, rows = refs[8:]
    core, z = sc[0], sc[2]
    for k in range(4):
        at = 2 * lax.rem(z + 4 - k, 4)
        for i in range(2):
            for a in range(6):
                rows[0, a, at + i] = mine[k][a, i]
                rows[1, a, at + i] = theirs[k][a, i]
    other = 1 - core
    for a in range(6):
        for r in range(OWN):
            low_own[a, r] = rows[core, a, 4 * core + r]
            high_own[a, r] = rows[other, a, 4 * core + r]
    for group, order, layout, near, far in (
        (core, ORDER_A, FIRST_A, near_a, far_a),
        (other, ORDER_B, FIRST_B, near_b, far_b),
    ):
        for a, name in order:
            offset, count = layout[name]
            for u in range(count):
                turn = core * (OWN - count) + u
                far[offset + u] = rows[group, a, 4 * core + turn]
                near[offset + u] = rows[group, a, 4 * other + turn]


def open_state(scalars, mine, theirs):
    vmem = pl.BlockSpec(memory_space=pltpu.VMEM)
    shapes = [(6, OWN)] * 2 + [(18,)] * 4
    return pl.pallas_call(
        open_state_kernel,
        out_shape=[jax.ShapeDtypeStruct(s + (CH, GW), BF) for s in shapes],
        in_specs=[pl.BlockSpec(memory_space=pltpu.SMEM)] + [vmem] * 8,
        out_specs=[vmem] * 6,
        scratch_shapes=[pltpu.VMEM((2, 6, 8, CH, GW), BF)],
        compiler_params=pltpu.CompilerParams(vmem_limit_bytes=16 << 20),
        name="open_state",
    )(scalars, *mine, *theirs)


def cut_result_kernel(sc, low, high, taken, *pieces):
    core, z = sc[0], sc[2]
    for k in range(4):
        to = lax.rem(z + k, 4)
        here = (to // 2) == core
        row = 2 * lax.rem(to, 2)
        for a in range(5):
            for i in range(2):
                own = jnp.where(core == 0, low[a, row + i], high[a, row + i])
                pieces[k][a, i] = jnp.where(here, own, taken[a, row + i])


def cut_result(scalars, low, high, taken):
    vmem = pl.BlockSpec(memory_space=pltpu.VMEM)
    return pl.pallas_call(
        cut_result_kernel,
        out_shape=[jax.ShapeDtypeStruct((5, 2, CH, GW), BF)] * 4,
        in_specs=[pl.BlockSpec(memory_space=pltpu.SMEM)] + [vmem] * 3,
        out_specs=[vmem] * 4,
        compiler_params=pltpu.CompilerParams(vmem_limit_bytes=8 << 20),
        name="cut_result",
    )(scalars, low, high, taken)


def close_result_kernel(sc, *refs):
    parts = refs[:4]
    hidden, cell, memory = refs[4:]
    z = sc[2]
    for k in range(4):
        seq = lax.rem(z + 4 - k, 4)
        for i in range(2):
            for a in range(2):
                hidden[a, seq, i] = parts[k][a, i]
                cell[a, seq, i] = parts[k][2 + a, i]
            memory[0, seq, i] = parts[k][4, i]


def close_result(scalars, parts):
    vmem = pl.BlockSpec(memory_space=pltpu.VMEM)
    shapes = ((2, 4, 2), (2, 4, 2), (1, 4, 2))
    return pl.pallas_call(
        close_result_kernel,
        out_shape=[jax.ShapeDtypeStruct(s + (CH, GW), BF) for s in shapes],
        in_specs=[pl.BlockSpec(memory_space=pltpu.SMEM)] + [vmem] * 4,
        out_specs=[vmem] * 3,
        compiler_params=pltpu.CompilerParams(vmem_limit_bytes=8 << 20),
        name="close_result",
    )(scalars, *parts)


def program(frames, hidden_in, cell_in, memory_in, w_x, w_h, w_m, w_o, w_last):
    core = lax.axis_index("layer")
    chip = lax.axis_index("rows")
    chips = lax.axis_size("rows")
    swap = [(0, 1), (1, 0)]
    across = []
    for i in range(chips):
        across.append((chips + i, i + 4 if i + 4 < chips else chips + (i ^ 1)))
        across.append((i, chips + i - 4 if i >= 4 else i ^ 1))

    def to_partner(value):
        return lax.ppermute(value, "layer", swap)

    def to_neighbour(value):
        return lax.ppermute(value, ("layer", "rows"), across)

    def around(value, k):
        turn = [(i, 4 * (i // 4) + (i + k) % 4) for i in range(chips)]
        return lax.ppermute(value, "rows", turn)

    scalars = jnp.stack([core, 8 * (chip // 4) + 4 * core, chip % 4]).astype(jnp.int32)
    turned = [jnp.swapaxes(w, 1, 2) for w in (w_x, w_m, w_o, w_last)]
    scalars, own_w = lax.optimization_barrier(
        (scalars, [turned[0], w_h, turned[1], turned[2], turned[3]])
    )
    other_w = [to_partner(w) for w in own_w]
    wa, wb, wc, wo = pack_weights(scalars, own_w, other_w)

    pieces = cut_state(scalars, frames, hidden_in, cell_in, memory_in)
    mine = [pieces[0]] + [None] * 3
    for k in (2, 1, 3):
        mine[k] = around(pieces[k], k)
    theirs = [to_partner(piece) for piece in mine]
    low_own, high_own, near_a, near_b, message_a, message_b = open_state(scalars, mine, theirs)
    far_a = to_neighbour(message_a)
    far_b = to_neighbour(message_b)

    base = {"sc": scalars, "wa": wa, "wb": wb, "wc": wc, "wo": wo}
    arrays = {"s00": low_own, "s01": high_own, "na": near_a, "fa": far_a, "nb": near_b, "fb": far_b}

    def first(letter, layout, field):
        offset, count = layout[field]
        return ("n" + letter, offset, "f" + letter, offset, count)

    kept = ("HB", "HT", "CB", "CT")
    halo = [{k: first("a", FIRST_A, k) for k in kept}, {k: first("b", FIRST_B, k) for k in kept}]
    states = ["s00", "s01"]
    own_m = ("s00", 4)
    halo_m = first("a", FIRST_A, "M")
    frame_field = (
        (("s00", 5), first("a", FIRST_A, "F0")),
        (("s01", 4), first("b", FIRST_B, "F1")),
        (("s01", 5), first("b", FIRST_B, "F2")),
    )
    steps = frames.shape[0]
    results = [None, None]
    for step in range(steps):
        x_field = frame_field[step]
        for half in range(2):
            send = 2 if step < steps - 1 else 1 - half
            fields = {k: ((states[half], SLOT[k]), halo[half][k]) for k in kept}
            fields["M"] = (own_m, halo_m)
            fields["X"] = x_field
            tag = f"{step}{half}"
            early = tag != "00"
            ahead = ("HB", "HT", "X") if half == 0 else ("HB", "HT")

            def gather(wanted, weights):
                used = {k: fields[k] for k in wanted}
                needed = {f[0][0] for f in used.values()}
                needed |= {f[1][i] for f in used.values() for i in (0, 2)}
                operands = {k: base[k] for k in ("sc",) + weights}
                operands.update({name: arrays[name] for name in sorted(needed)})
                return used, operands

            plan = {"half": half, "layer": 2 * half, "send": send, "early": early}
            if early:
                used, operands = gather(ahead, ("wa", "wb"))
                sums = run_early(operands, dict(plan, fields=used))
                used, operands = gather(
                    [k for k in fields if k not in ahead], ("wb", "wc", "wo")
                )
                operands.update(sums0=sums[0], sums1=sums[1])
            else:
                used, operands = gather(fields, ("wa", "wb", "wc", "wo"))
            plan["fields"] = used
            if not send:
                plan["lower"] = states[0]
                operands[states[0]] = arrays[states[0]]
            outs = run_phase(operands, plan)
            results[half] = outs["state"]
            states[half] = "state" + tag
            arrays["state" + tag] = outs["state"]
            own_m = ("state" + tag, SLOT["M"])
            if send:
                arrays["soon" + tag] = to_neighbour(outs["soon"])
                arrays["near" + tag] = to_partner(outs["near"])
                near_at = both(half)
                for k, (o, n) in SOON[half].items():
                    spec = ("near" + tag, near_at[k][0], "soon" + tag, o, n)
                    if k == "M":
                        halo_m = spec
                    else:
                        x_field = (("state" + tag, SLOT["HT"]), spec)
                        halo[half][k] = spec
            if send > 1:
                arrays["late" + tag] = to_neighbour(outs["late"])
                for k, (o, n) in LATE[half].items():
                    halo[half][k] = ("near" + tag, near_at[k][0], "late" + tag, o, n)

    taken = to_partner(outs["give"])
    pieces = cut_result(scalars, results[0], results[1], taken)
    done = [pieces[0]] + [None] * 3
    for k in (2, 1, 3):
        done[k] = around(pieces[k], k)
    return tuple(close_result(scalars, done))


def solution(mesh):
    return jax.shard_map(
        program,
        mesh=mesh,
        in_specs=(
            P(None, None, "rows", None, None),
            P("layer", None, "rows", None, None),
            P("layer", None, "rows", None, None),
            P(None, "rows", None, None),
            P("layer", None, None),
            P("layer", None, None),
            P("layer", None, None),
            P("layer", None, None),
            P("layer", None, None),
        ),
        out_specs=(
            P("layer", None, "rows", None, None),
            P("layer", None, "rows", None, None),
            P("layer", None, "rows", None, None),
        ),
        check_vma=False,
    )
```

```python
import functools

import jax
import jax.numpy as jnp
from jax import lax
from jax.experimental import pallas as pl
from jax.experimental.pallas import tpu as pltpu
from jax.sharding import PartitionSpec as P


LAYER, ROWS = "layer", "rows"
CH = 64
GW = 128
OWN = 4
BF = jnp.bfloat16
F32 = jnp.float32

FIRST_A = {"HT": (0, 2), "M": (2, 4), "HB": (6, 4), "CB": (10, 3), "CT": (13, 1), "F0": (14, 4)}
FIRST_B = {"HT": (0, 2), "HB": (2, 4), "CB": (6, 3), "CT": (9, 1), "F1": (10, 4), "F2": (14, 4)}
SOON = ({"HT": (0, 4), "M": (4, 4)}, {"M": (0, 4)})
LATE = (
    {"HB": (0, 4), "CB": (4, 3), "CT": (7, 1)},
    {"HT": (0, 2), "HB": (2, 4), "CB": (6, 3), "CT": (9, 1)},
)
SLOT = {"HB": 0, "HT": 1, "CB": 2, "CT": 3, "M": 4}
REACH = (3, 1)


def units(layout):
    return sum(count for _, count in layout.values())


def both(half):
    shift = units(SOON[half])
    near = dict(SOON[half])
    near.update({k: (o + shift, n) for k, (o, n) in LATE[half].items()})
    return near


def sigmoid(v):
    return 0.5 * jnp.tanh(0.5 * v) + 0.5


def taps_of(row):
    lane = lax.broadcasted_iota(jnp.int32, row.shape, 1)
    zero = jnp.zeros_like(row)
    before = jnp.where(lane == 0, zero, pltpu.roll(row, 1, 1))
    after = jnp.where(lane == GW - 1, zero, pltpu.roll(row, GW - 1, 1))
    return jnp.concatenate([before, row, after], axis=0)


def accessors(ref, fields):
    core = ref["sc"][0]
    top = ref["sc"][1]
    first_core = core == 0

    def keep(row, value):
        if 0 <= row < OWN:
            return value
        g = top + row
        return jnp.where(jnp.logical_and(g >= 0, g < 128), value, jnp.zeros_like(value))

    def fetch(field, row):
        (own, slot), (near, near_at, far, far_at, count) = fields[field]
        if 0 <= row < OWN:
            return ref[own][slot, row]
        if row < 0:
            unit = count + row
            value = jnp.where(first_core, ref[far][far_at + unit], ref[near][near_at + unit])
        else:
            unit = row - OWN
            value = jnp.where(first_core, ref[near][near_at + unit], ref[far][far_at + unit])
        return keep(row, value)

    return first_core, keep, fetch


def stacked(bufs, q):
    cols = [
        jnp.concatenate([buf[i + a] for buf in bufs for a in range(3)], axis=0) for i in (q, q + 1)
    ]
    return jnp.concatenate(cols, axis=1)


def early_kernel(plan, *refs):
    names, half = plan["names"], plan["half"]
    ref = dict(zip(names, refs))
    sums, tx, th, th2 = refs[len(names) : len(names) + 2], *refs[len(names) + 2 :]
    _, _, fetch = accessors(ref, plan["fields"])
    filled = set()

    def fill(buf, field, reach, upto):
        for i in range(upto):
            if (field, i) not in filled:
                filled.add((field, i))
                buf[i] = taps_of(fetch(field, i - reach))

    for index in range(2):
        layer = plan["base"] + index
        for q in range(0, OWN + 2 * REACH[index], 2):
            with_x = half == 0 and index == 0
            fill((th, th2)[index], ("HB", "HT")[index], REACH[index] + 1, q + 4)
            h = stacked([(th, th2)[index]], q)
            own = jnp.dot(ref["wa"][layer], h[0:512], preferred_element_type=F32)
            if with_x:
                fill(tx, "X", 4, q + 4)
                x = stacked([tx], q)
                shared = jnp.dot(
                    ref["wb"][layer, :, 0:640],
                    jnp.concatenate([x, h[512:576]], axis=0),
                    preferred_element_type=F32,
                )
                sums[index][q // 2, 0:256] = own + shared[0:256]
                sums[index][q // 2, 256:448] = shared[256:448]
            else:
                rest = jnp.concatenate([jnp.zeros((64, 2 * GW), BF), h[512:576]], axis=0)
                sums[index][q // 2] = own + jnp.dot(
                    ref["wb"][layer, 0:256, 512:640], rest, preferred_element_type=F32
                )


def phase_kernel(plan, *refs):
    names = plan["names"]
    outs = plan["outs"]
    n_in = len(names)
    ref = dict(zip(names, refs[:n_in]))
    out = dict(zip(outs, refs[n_in : n_in + len(outs)]))
    tx, th, tm, tx2, th2, tm2, yb, ob, yb2, ob2 = refs[n_in + len(outs) :]
    state_out = out["state"]
    first_core, keep, fetch = accessors(ref, plan["fields"])

    rows_of = [list(range(-reach, OWN + reach)) for reach in REACH]
    bufs = ((tx, th, tm, yb, ob), (tx2, th2, tm2.at[1:9], yb2, ob2))
    filled = set()

    def fill(buf, key, field, reach, upto):
        for i in range(upto):
            if (key, i) not in filled:
                filled.add((key, i))
                buf[i] = taps_of(fetch(field, i - reach))

    early = plan["early"]

    def matmuls(index, q):
        bx, bh, bm, _, _ = bufs[index]
        layer = plan["base"] + index
        add = lambda w, rhs: jnp.dot(w, rhs, preferred_element_type=F32)
        if index == 0:
            fill(tm, "m", "M", 4, q + 4)
            if not (early and plan["half"] == 0):
                fill(tx, "x", "X", 4, q + 4)
        m = stacked([bm], q)
        rest = add(ref["wc"][layer], m[128:576])
        if early and plan["half"] == 0 and index == 0:
            acc2 = rest + add(ref["wb"][layer, 256:448, 640:768], m[0:128])
            return ref["sums0"][q // 2, 0:256], acc2 + ref["sums0"][q // 2, 256:448]
        if early:
            h_rest = jnp.zeros((64, 2 * GW), BF)
            own = ref[f"sums{index}"][q // 2]
        else:
            if index == 0:
                fill(th, "h", "HB", 4, q + 4)
            else:
                fill(th2, "h2", "HT", 2, q + 4)
            h = stacked([bh], q)
            h_rest = h[512:576]
            own = add(ref["wa"][layer], h[0:512])
        shared = add(
            ref["wb"][layer], jnp.concatenate([stacked([bx], q), h_rest, m[0:128]], axis=0)
        )
        return shared[0:256] + own, shared[256:448] + rest

    def gates(index, q, acc1, acc2):
        _, _, _, y_buf, o_buf = bufs[index]
        rows = rows_of[index]
        pair = (rows[q], rows[q + 1])
        c_field = "CT" if index else "CB"
        c_prev = jnp.concatenate([fetch(c_field, row) for row in pair], axis=1).astype(F32)
        if index:
            m_rows = [tm2[row + 3, 64:128] for row in pair]
        else:
            m_rows = [tm[row + 4, 64:128] for row in pair]
        m_prev = jnp.concatenate(m_rows, axis=1).astype(F32)
        c_new = sigmoid(acc1[64:128] + 1.0) * c_prev + sigmoid(acc1[0:64]) * jnp.tanh(acc1[128:192])
        m_new = sigmoid(acc2[64:128] + 1.0) * m_prev + sigmoid(acc2[0:64]) * jnp.tanh(acc2[128:192])
        c_new = c_new.astype(BF)
        m_new = m_new.astype(BF)
        lanes = slice(q * GW, (q + 2) * GW)
        o_buf[:, lanes] = acc1[192:256]
        blocks = []
        for j, row in enumerate(pair):
            c_row = keep(row, c_new[:, j * GW : (j + 1) * GW])
            m_row = keep(row, m_new[:, j * GW : (j + 1) * GW])
            if 0 <= row < OWN:
                state_out[SLOT[c_field], row] = c_row
                if index:
                    state_out[SLOT["M"], row] = m_row
            c_taps = taps_of(c_row)
            m_taps = taps_of(m_row)
            if not index:
                tm2[row + 3] = m_taps
            blocks.append(
                jnp.concatenate(
                    [t[64 * b : 64 * b + 64] for b in range(3) for t in (c_taps, m_taps)], axis=0
                )
            )
        y_buf[:, lanes] = jnp.dot(
            ref["wo"][plan["base"] + index],
            jnp.concatenate(blocks, axis=1),
            preferred_element_type=F32,
        )

    def hidden(index, q):
        _, _, _, y_buf, o_buf = bufs[index]
        lanes = slice(q * GW, (q + 1) * GW)
        gate = (
            o_buf[:, lanes]
            + y_buf[0:64, (q - 1) * GW : q * GW]
            + y_buf[64:128, lanes]
            + y_buf[128:192, (q + 1) * GW : (q + 2) * GW]
        )
        h_new = (sigmoid(gate) * jnp.tanh(y_buf[192:256, lanes])).astype(BF)
        row = rows_of[index][q]
        h_new = keep(row, h_new)
        if 0 <= row < OWN:
            state_out[SLOT["HT" if index else "HB"], row] = h_new
        if not index:
            tx2[row + 2] = taps_of(h_new)

    def finish(index, q, accs):
        gates(index, q, *accs)
        for h in (q - 1, q):
            if h >= 1:
                hidden(index, h)

    tasks = [(i, q) for i in range(2) for q in range(0, len(rows_of[i]), 2)]
    waiting = None
    for task in tasks:
        accs = matmuls(*task)
        if waiting is not None:
            finish(*waiting)
        waiting = task + (accs,)
    finish(*waiting)

    def send(target, layout, last_rows_if):
        for field, (offset, count) in layout.items():
            for u in range(count):
                low = state_out[SLOT[field], u]
                high = state_out[SLOT[field], OWN - count + u]
                target[offset + u] = jnp.where(last_rows_if, high, low)

    half = plan["half"]
    if "give" in out:
        lower, slots = ref[plan["lower"]], out["give"].shape[0]
        for slot in range(slots):
            for row in range(OWN):
                out["give"][slot, row] = jnp.where(
                    first_core, state_out[slot, row], lower[slot, row]
                )
    if "near" in out:
        send(out["near"], both(half) if "late" in out else SOON[half], first_core)
    if "soon" in out:
        send(out["soon"], SOON[half], jnp.logical_not(first_core))
    if "late" in out:
        send(out["late"], LATE[half], jnp.logical_not(first_core))


def run_early(operands, plan):
    names = list(operands)
    plan = dict(plan, names=names)
    height = 448 if plan["half"] == 0 else 256
    taps = (3 * CH, GW)
    return pl.pallas_call(
        functools.partial(early_kernel, plan),
        out_shape=[
            jax.ShapeDtypeStruct((5, height, 2 * GW), F32),
            jax.ShapeDtypeStruct((3, 256, 2 * GW), F32),
        ],
        in_specs=[
            pl.BlockSpec(memory_space=pltpu.SMEM if name == "sc" else pltpu.VMEM) for name in names
        ],
        out_specs=[pl.BlockSpec(memory_space=pltpu.VMEM)] * 2,
        scratch_shapes=[
            pltpu.VMEM((12,) + taps, BF), pltpu.VMEM((12,) + taps, BF), pltpu.VMEM((8,) + taps, BF)
        ],
        compiler_params=pltpu.CompilerParams(vmem_limit_bytes=12 << 20),
        name="early_sums",
    )(*[operands[name] for name in names])


def run_phase(operands, plan):
    names = list(operands)
    plan = dict(plan, names=names)
    unit = (CH, GW)
    half = plan["half"]
    sizes = {"state": (5, OWN) + unit}
    if plan["send"]:
        far = {"soon": units(SOON[half])}
        if plan["send"] > 1:
            far["late"] = units(LATE[half])
        sizes["near"] = (sum(far.values()),) + unit
        sizes.update({k: (n,) + unit for k, n in far.items()})
    else:
        sizes["give"] = sizes["state"]
    plan["outs"] = list(sizes)
    in_specs = [
        pl.BlockSpec(memory_space=pltpu.SMEM if name == "sc" else pltpu.VMEM) for name in names
    ]
    results = pl.pallas_call(
        functools.partial(phase_kernel, plan),
        out_shape=[jax.ShapeDtypeStruct(s, BF) for s in sizes.values()],
        in_specs=in_specs,
        out_specs=[pl.BlockSpec(memory_space=pltpu.VMEM) for _ in sizes],
        scratch_shapes=[
            pltpu.VMEM((12, 3 * CH, GW), BF),
            pltpu.VMEM((12, 3 * CH, GW), BF),
            pltpu.VMEM((12, 3 * CH, GW), BF),
            pltpu.VMEM((8, 3 * CH, GW), BF),
            pltpu.VMEM((8, 3 * CH, GW), BF),
            pltpu.VMEM((10, 3 * CH, GW), BF),
            pltpu.VMEM((4 * CH, 10 * GW), F32),
            pltpu.VMEM((CH, 10 * GW), F32),
            pltpu.VMEM((4 * CH, 6 * GW), F32),
            pltpu.VMEM((CH, 6 * GW), F32),
        ],
        compiler_params=pltpu.CompilerParams(vmem_limit_bytes=24 << 20),
        name="two_layers",
    )(*[operands[name] for name in names])
    return dict(zip(sizes, results))


def in_hbm(*values):
    return [pltpu.with_memory_space_constraint(v, pltpu.HBM) for v in values]


def pack_weights_kernel(sc, *refs):
    sources, (wa, wb, wc, wo) = refs[:10], refs[10:14]
    inputs, sems = refs[14:24], refs[24]
    core = sc[0]
    copies = [pltpu.make_async_copy(s, t, sems.at[i]) for i, (s, t) in enumerate(zip(sources, inputs))]
    for c in copies:
        c.start()
    for group in range(2):
        for c in copies[5 * group : 5 * group + 5]:
            c.wait()
        x, h, m, o, last = inputs[5 * group : 5 * group + 5]
        first = 2 * core if group == 0 else 2 - 2 * core
        for l in range(2):
            at = first + l
            xt = x[l]
            ht = jnp.transpose(h[l])
            mt = m[l]
            ot = o[l]
            wa[at] = ht[:, 0:512]
            wc[at] = mt[:, 128:576]
            gate_rows = jnp.concatenate([xt[0:192], xt[384:448]], axis=0)
            wb[at, 0:256, 0:512] = gate_rows[:, 0:512]
            wb[at, 0:256, 512:640] = jnp.concatenate([gate_rows[:, 512:576], ht[:, 512:576]], axis=1)
            wb[at, 0:256, 640:768] = jnp.zeros((256, 128), BF)
            wb[at, 256:448, 0:512] = xt[192:384, 0:512]
            wb[at, 256:448, 512:640] = jnp.concatenate(
                [xt[192:384, 512:576], jnp.zeros((192, 64), BF)], axis=1
            )
            wb[at, 256:448, 640:768] = mt[:, 0:128]
            for a in range(3):
                wo[at, 64 * a : 64 * a + 64] = ot[:, 384 * a : 384 * a + 384]
            wo[at, 192:256, 0:128] = jnp.zeros((64, 128), BF)
            wo[at, 192:256, 128:256] = last[l]
            wo[at, 192:256, 256:384] = jnp.zeros((64, 128), BF)


def pack_weights(scalars, own, other):
    shapes = ((4, 256, 512), (4, 448, 768), (4, 192, 448), (4, 256, 384))
    vmem = pl.BlockSpec(memory_space=pltpu.VMEM)
    return pl.pallas_call(
        pack_weights_kernel,
        out_shape=[jax.ShapeDtypeStruct(s, BF) for s in shapes],
        in_specs=[pl.BlockSpec(memory_space=pltpu.SMEM)]
        + [pl.BlockSpec(memory_space=pltpu.HBM)] * 10,
        out_specs=[vmem] * 4,
        scratch_shapes=[pltpu.VMEM(w.shape, BF) for w in (*own, *other)]
        + [pltpu.SemaphoreType.DMA((10,))],
        compiler_params=pltpu.CompilerParams(vmem_limit_bytes=32 << 20),
        name="pack_weights",
    )(scalars, *in_hbm(*own), *other)


def cut_state_kernel(sc, *refs):
    sources, pieces, copied, sems = refs[:4], refs[4:8], refs[8:12], refs[12]
    copies = [pltpu.make_async_copy(s, t, sems.at[i]) for i, (s, t) in enumerate(zip(sources, copied))]
    for c in copies:
        c.start()
    for c in copies:
        c.wait()
    frames, hidden, cell, memory = copied
    first_core, z = sc[0] == 0, sc[2]
    for k in range(4):
        seq = lax.rem(z + k, 4)
        for i in range(2):
            for l in range(2):
                pieces[k][l, i] = hidden[l, seq, i]
                pieces[k][2 + l, i] = cell[l, seq, i]
            pieces[k][4, i] = jnp.where(first_core, memory[seq, i], frames[1, seq, i])
            pieces[k][5, i] = jnp.where(first_core, frames[0, seq, i], frames[2, seq, i])


def cut_state(scalars, frames, hidden, cell, memory):
    vmem = pl.BlockSpec(memory_space=pltpu.VMEM)
    return pl.pallas_call(
        cut_state_kernel,
        out_shape=[jax.ShapeDtypeStruct((6, 2, CH, GW), BF)] * 4,
        in_specs=[pl.BlockSpec(memory_space=pltpu.SMEM)]
        + [pl.BlockSpec(memory_space=pltpu.HBM)] * 4,
        out_specs=[vmem] * 4,
        scratch_shapes=[pltpu.VMEM(v.shape, BF) for v in (frames, hidden, cell, memory)]
        + [pltpu.SemaphoreType.DMA((4,))],
        compiler_params=pltpu.CompilerParams(vmem_limit_bytes=8 << 20),
        name="cut_state",
    )(scalars, *in_hbm(frames, hidden, cell, memory))


ORDER_A = ((1, "HT"), (4, "M"), (0, "HB"), (2, "CB"), (3, "CT"), (5, "F0"))
ORDER_B = ((1, "HT"), (0, "HB"), (2, "CB"), (3, "CT"), (4, "F1"), (5, "F2"))


def open_state_kernel(sc, *refs):
    mine, theirs = refs[:4], refs[4:8]
    low_own, high_own, near_a, near_b, far_a, far_b, rows = refs[8:]
    core, z = sc[0], sc[2]
    for k in range(4):
        at = 2 * lax.rem(z + 4 - k, 4)
        for i in range(2):
            for a in range(6):
                rows[0, a, at + i] = mine[k][a, i]
                rows[1, a, at + i] = theirs[k][a, i]
    other = 1 - core
    for a in range(6):
        for r in range(OWN):
            low_own[a, r] = rows[core, a, 4 * core + r]
            high_own[a, r] = rows[other, a, 4 * core + r]
    for group, order, layout, near, far in (
        (core, ORDER_A, FIRST_A, near_a, far_a),
        (other, ORDER_B, FIRST_B, near_b, far_b),
    ):
        for a, name in order:
            offset, count = layout[name]
            for u in range(count):
                turn = core * (OWN - count) + u
                far[offset + u] = rows[group, a, 4 * core + turn]
                near[offset + u] = rows[group, a, 4 * other + turn]


def open_state(scalars, mine, theirs):
    vmem = pl.BlockSpec(memory_space=pltpu.VMEM)
    shapes = [(6, OWN)] * 2 + [(18,)] * 4
    return pl.pallas_call(
        open_state_kernel,
        out_shape=[jax.ShapeDtypeStruct(s + (CH, GW), BF) for s in shapes],
        in_specs=[pl.BlockSpec(memory_space=pltpu.SMEM)] + [vmem] * 8,
        out_specs=[vmem] * 6,
        scratch_shapes=[pltpu.VMEM((2, 6, 8, CH, GW), BF)],
        compiler_params=pltpu.CompilerParams(vmem_limit_bytes=16 << 20),
        name="open_state",
    )(scalars, *mine, *theirs)


def cut_result_kernel(sc, low, high, taken, *pieces):
    core, z = sc[0], sc[2]
    for k in range(4):
        to = lax.rem(z + k, 4)
        here = (to // 2) == core
        row = 2 * lax.rem(to, 2)
        for a in range(5):
            for i in range(2):
                own = jnp.where(core == 0, low[a, row + i], high[a, row + i])
                pieces[k][a, i] = jnp.where(here, own, taken[a, row + i])


def cut_result(scalars, low, high, taken):
    vmem = pl.BlockSpec(memory_space=pltpu.VMEM)
    return pl.pallas_call(
        cut_result_kernel,
        out_shape=[jax.ShapeDtypeStruct((5, 2, CH, GW), BF)] * 4,
        in_specs=[pl.BlockSpec(memory_space=pltpu.SMEM)] + [vmem] * 3,
        out_specs=[vmem] * 4,
        compiler_params=pltpu.CompilerParams(vmem_limit_bytes=8 << 20),
        name="cut_result",
    )(scalars, low, high, taken)


def close_result_kernel(sc, *refs):
    parts = refs[:4]
    hidden, cell, memory = refs[4:]
    z = sc[2]
    for k in range(4):
        seq = lax.rem(z + 4 - k, 4)
        for i in range(2):
            for a in range(2):
                hidden[a, seq, i] = parts[k][a, i]
                cell[a, seq, i] = parts[k][2 + a, i]
            memory[0, seq, i] = parts[k][4, i]


def close_result(scalars, parts):
    vmem = pl.BlockSpec(memory_space=pltpu.VMEM)
    shapes = ((2, 4, 2), (2, 4, 2), (1, 4, 2))
    return pl.pallas_call(
        close_result_kernel,
        out_shape=[jax.ShapeDtypeStruct(s + (CH, GW), BF) for s in shapes],
        in_specs=[pl.BlockSpec(memory_space=pltpu.SMEM)] + [vmem] * 4,
        out_specs=[vmem] * 3,
        compiler_params=pltpu.CompilerParams(vmem_limit_bytes=8 << 20),
        name="close_result",
    )(scalars, *parts)


def program(frames, hidden_in, cell_in, memory_in, w_x, w_h, w_m, w_o, w_last):
    core = lax.axis_index(LAYER)
    chip = lax.axis_index(ROWS)
    chips = lax.axis_size(ROWS)
    swap = [(0, 1), (1, 0)]
    across = []
    for i in range(chips):
        across.append((chips + i, i + 4 if i + 4 < chips else chips + (i ^ 1)))
        across.append((i, chips + i - 4 if i >= 4 else i ^ 1))

    def to_partner(value):
        return lax.ppermute(value, LAYER, swap)

    def to_neighbour(value):
        return lax.ppermute(value, (LAYER, ROWS), across)

    def around(value, k):
        turn = [(i, 4 * (i // 4) + (i + k) % 4) for i in range(chips)]
        return lax.ppermute(value, ROWS, turn)

    scalars = jnp.stack([core, 8 * (chip // 4) + 4 * core, chip % 4]).astype(jnp.int32)
    turned = [jnp.swapaxes(w, 1, 2) for w in (w_x, w_m, w_o, w_last)]
    scalars, own_w = lax.optimization_barrier(
        (scalars, [turned[0], w_h, turned[1], turned[2], turned[3]])
    )
    other_w = [to_partner(w) for w in own_w]
    wa, wb, wc, wo = pack_weights(scalars, own_w, other_w)

    pieces = cut_state(scalars, frames, hidden_in, cell_in, memory_in)
    mine = [pieces[0]] + [None] * 3
    for k in (2, 1, 3):
        mine[k] = around(pieces[k], k)
    theirs = [to_partner(piece) for piece in mine]
    low_own, high_own, near_a, near_b, message_a, message_b = open_state(scalars, mine, theirs)
    far_a = to_neighbour(message_a)
    far_b = to_neighbour(message_b)

    base = {"sc": scalars, "wa": wa, "wb": wb, "wc": wc, "wo": wo}
    arrays = {"s00": low_own, "s01": high_own, "na": near_a, "fa": far_a, "nb": near_b, "fb": far_b}

    def first(letter, layout, field):
        offset, count = layout[field]
        return ("n" + letter, offset, "f" + letter, offset, count)

    kept = ("HB", "HT", "CB", "CT")
    halo = [{k: first("a", FIRST_A, k) for k in kept}, {k: first("b", FIRST_B, k) for k in kept}]
    states = ["s00", "s01"]
    own_m = ("s00", 4)
    halo_m = first("a", FIRST_A, "M")
    frame_field = (
        (("s00", 5), first("a", FIRST_A, "F0")),
        (("s01", 4), first("b", FIRST_B, "F1")),
        (("s01", 5), first("b", FIRST_B, "F2")),
    )
    steps = frames.shape[0]
    results = [None, None]
    for step in range(steps):
        x_field = frame_field[step]
        for half in range(2):
            send = 2 if step < steps - 1 else 1 - half
            fields = {k: ((states[half], SLOT[k]), halo[half][k]) for k in kept}
            fields["M"] = (own_m, halo_m)
            fields["X"] = x_field
            tag = f"{step}{half}"
            early = tag != "00"
            ahead = ("HB", "HT", "X") if half == 0 else ("HB", "HT")

            def gather(wanted, weights):
                used = {k: fields[k] for k in wanted}
                needed = {f[0][0] for f in used.values()}
                needed |= {f[1][i] for f in used.values() for i in (0, 2)}
                operands = {k: base[k] for k in ("sc",) + weights}
                operands.update({name: arrays[name] for name in sorted(needed)})
                return used, operands

            plan = {"half": half, "base": 2 * half, "send": send, "early": early}
            if early:
                used, operands = gather(ahead, ("wa", "wb"))
                sums = run_early(operands, dict(plan, fields=used))
                used, operands = gather(
                    [k for k in fields if k not in ahead], ("wb", "wc", "wo")
                )
                operands.update(sums0=sums[0], sums1=sums[1])
            else:
                used, operands = gather(fields, ("wa", "wb", "wc", "wo"))
            plan["fields"] = used
            if not send:
                plan["lower"] = states[0]
                operands[states[0]] = arrays[states[0]]
            outs = run_phase(operands, plan)
            results[half] = outs["state"]
            states[half] = "state" + tag
            arrays["state" + tag] = outs["state"]
            own_m = ("state" + tag, SLOT["M"])
            if send:
                arrays["soon" + tag] = to_neighbour(outs["soon"])
                arrays["near" + tag] = to_partner(outs["near"])
                near_at = both(half)
                for k, (o, n) in SOON[half].items():
                    spec = ("near" + tag, near_at[k][0], "soon" + tag, o, n)
                    if k == "M":
                        halo_m = spec
                    else:
                        x_field = (("state" + tag, SLOT["HT"]), spec)
                        halo[half][k] = spec
            if send > 1:
                arrays["late" + tag] = to_neighbour(outs["late"])
                for k, (o, n) in LATE[half].items():
                    halo[half][k] = ("near" + tag, near_at[k][0], "late" + tag, o, n)

    taken = to_partner(outs["give"])
    pieces = cut_result(scalars, results[0], results[1], taken)
    done = [pieces[0]] + [None] * 3
    for k in (2, 1, 3):
        done[k] = around(pieces[k], k)
    return tuple(close_result(scalars, done))


def solution(mesh):
    return jax.shard_map(
        program,
        mesh=mesh,
        in_specs=(
            P(None, None, ROWS, None, None),
            P(LAYER, None, ROWS, None, None),
            P(LAYER, None, ROWS, None, None),
            P(None, ROWS, None, None),
            P(LAYER, None, None),
            P(LAYER, None, None),
            P(LAYER, None, None),
            P(LAYER, None, None),
            P(LAYER, None, None),
        ),
        out_specs=(
            P(LAYER, None, ROWS, None, None),
            P(LAYER, None, ROWS, None, None),
            P(LAYER, None, ROWS, None, None),
        ),
        check_vma=False,
    )
```
